512 devices in a mesh: node: 64 (over y_hi, z, x), head: 8 (over y_lo, core).
Axes of the slice: x: 4, y: 8 (y_hi: 2, y_lo: 4; y = y_hi * 4 + y_lo), z: 8, core: 2. Of those that a mesh axis runs over, the one named last changes fastest.
Arguments:
- features: bfloat16 [8192, 128], P('node'), may hold values from -1201 to 1201
- proj_weight: bfloat16 [128, 1024], P(None, 'head'), may hold values from -1 to 1
- score_source: float32 [8, 128], P('head'), may hold values from -1 to 1
- score_target: float32 [8, 128], P('head'), may hold values from -1 to 1
- out_weight: bfloat16 [1024, 256], P('head'), may hold values from -0.1875 to 0.1875
- presence: int32 [64, 64], P('node'), may hold values from 0 to 1, as said below
- tile_masks: int32 [64, 16, 128, 128], P('node'), may hold values 0 or 1
Outputs:
- mixed: bfloat16 [8192, 256], P('node')
The draws below stay inside these ranges and needn't reach their ends.
Inputs may be any that keep to these rules, and one draw needn't show every extreme that they name: Each row holds exactly 16 ones; tile_masks[r, k] belongs to the k-th present tile of row r of presence, counted in ascending order of tile.
All inputs are finite; a program needn't handle non-finite values. No bound on the sum of `tile_masks` on one device may be relied on, other than what follows from the above.
Results may differ from the reference program's by a relative error of at most 0.015.
Values may be sent and summed in bfloat16 or wider, within the bound.
No kernel may reach another device: no remote copies, remote signals or barrier semaphores. Data moves between devices by JAX's collectives and lax.ppermute only.
A program may use at most 64 MiB of HBM per device.

```python
import math
import jax
import jax.numpy as jnp
from jax import lax

D_IN = 128
HEADS = 8
HD = 128
OUT = 256
TILE = 128
NODES = 8192
TILE_COUNT = 64
TILE_SLOTS = 16


def shared_weights(key):
    weight = jax.random.truncated_normal(jax.random.fold_in(key, 31), -4.0, 4.0, (D_IN, HEADS * HD), jnp.float32) / math.sqrt(D_IN)
    source_vec = jax.random.truncated_normal(jax.random.fold_in(key, 32), -4.0, 4.0, (HEADS, HD), jnp.float32) / math.sqrt(HD)
    target_vec = jax.random.truncated_normal(jax.random.fold_in(key, 33), -4.0, 4.0, (HEADS, HD), jnp.float32) / math.sqrt(HD)
    return (weight, source_vec, target_vec)


def draw_proj_weight(key, part):
    return shared_weights(key)[0].astype(jnp.bfloat16)


def draw_score_source(key, part):
    return shared_weights(key)[1]


def draw_score_target(key, part):
    return shared_weights(key)[2]


def draw_features(key, part):
    base = jax.random.truncated_normal(jax.random.fold_in(key, 34), -6.0, 6.0, (NODES, D_IN), jnp.float32)
    return base.astype(jnp.bfloat16)


def draw_presence(key, part):
    noise_key, favour_key = jax.random.split(jax.random.fold_in(key, 21))
    noise = jax.random.randint(noise_key, (TILE_COUNT, TILE_COUNT), 0, 65536, dtype=jnp.int32)
    favour = jax.random.randint(favour_key, (1, TILE_COUNT), 1, 5, dtype=jnp.int32)
    ranking = noise * favour * TILE_COUNT + jnp.arange(TILE_COUNT, dtype=jnp.int32)[None, :]
    cutoff = lax.top_k(ranking, TILE_SLOTS)[0][:, TILE_SLOTS - 1:TILE_SLOTS]
    return (ranking >= cutoff).astype(jnp.int32)


def plant(array, stream_key, least, top_value):
    longest = array.shape.index(max(array.shape))
    spots = []
    for shift in (0, 1):
        where = [jax.random.randint(jax.random.fold_in(stream_key, axis), (), 0, length) for axis, length in enumerate(array.shape)]
        where[longest] = (where[longest] + shift) % array.shape[longest]
        spots.append(tuple(where))
    return array.at[spots[0]].set(least).at[spots[1]].set(top_value)


def block_scale(key, dims, pieces, smallest, high):
    def one(dim, blocks):
        steps = jax.random.uniform(jax.random.fold_in(jax.random.fold_in(key, 6), dim), (blocks,), jnp.float32, smallest / len(pieces), high / len(pieces))
        return jnp.repeat(jnp.exp(steps), dims[dim] // blocks).reshape((-1,) + (1,) * (len(dims) - dim - 1))

    loudness = one(*pieces[0])
    for cut in pieces[1:]:
        loudness = loudness * one(*cut)
    return loudness


def centred(stream_key, extent, deviation, most, cuts=(), kind=jnp.bfloat16):
    gain = block_scale(stream_key, extent, cuts, -0.22, 0.18) if cuts else 1.0
    values = jax.random.normal(stream_key, extent, jnp.float32) * deviation * gain
    return jnp.minimum(jnp.maximum(values, -most), most).astype(kind)


def setup_inputs(seed: int = 0) -> dict:
    arg_keys = jax.random.split(jax.random.key(seed), 8)
    return {
        "features": draw_features(jax.random.fold_in(arg_keys[7], 71), 0),
        "proj_weight": draw_proj_weight(jax.random.fold_in(arg_keys[7], 71), 0),
        "score_source": draw_score_source(jax.random.fold_in(arg_keys[7], 71), 0),
        "score_target": draw_score_target(jax.random.fold_in(arg_keys[7], 71), 0),
        "out_weight": centred(arg_keys[4], (HEADS * HD, OUT), (HEADS * HD) ** -0.5, 0.1875, ((0, 8),)),
        "presence": draw_presence(jax.random.fold_in(arg_keys[7], 71), 0),
        "tile_masks": plant((jax.random.randint(arg_keys[6], (TILE_COUNT, TILE_SLOTS, TILE, TILE), 0, 8) < 1).astype(jnp.int32), jax.random.fold_in(arg_keys[6], 1), 0, 1),
    }


def leaky_relu(values):
    return jnp.where(values > 0, values, 0.2 * values)


def reference(features, proj_weight, score_source, score_target, out_weight, presence, tile_masks):
    projected = jnp.dot(features, proj_weight, preferred_element_type=jnp.float32).astype(jnp.bfloat16)
    values = lax.optimization_barrier(projected).astype(jnp.float32).reshape(NODES, HEADS, HD)
    target_terms = jnp.sum(values * score_target[None], axis=-1)
    source_terms = jnp.sum(values * score_source[None], axis=-1)
    tile_lanes = jnp.arange(TILE, dtype=jnp.int32)

    def one_tile(row_tile):
        present_ids = jnp.nonzero(presence[row_tile], size=TILE_SLOTS)[0].astype(jnp.int32)
        source_ids = (present_ids[:, None] * TILE + tile_lanes[None, :]).reshape(TILE_SLOTS * TILE)
        target_ids = row_tile * TILE + tile_lanes
        tile_bits = jnp.transpose(tile_masks[row_tile], (1, 0, 2)).reshape(TILE, TILE_SLOTS * TILE)
        linked = (tile_bits == 1) & (source_ids[None, :] != target_ids[:, None])
        edge_scores = leaky_relu(target_terms[target_ids][:, None, :] + source_terms[source_ids][None, :, :])
        self_score = leaky_relu(target_terms[target_ids] + source_terms[target_ids])
        masked = jnp.where(linked[:, :, None], edge_scores, -jnp.inf)
        row_peak = jnp.maximum(jnp.max(masked, axis=1), self_score)
        edge_weights = jnp.where(linked[:, :, None], jnp.exp(edge_scores - row_peak[:, None, :]), 0.0)
        self_weight = jnp.exp(self_score - row_peak)
        denominator = jnp.sum(edge_weights, axis=1) + self_weight
        rounded = lax.optimization_barrier(edge_weights.astype(jnp.bfloat16)).astype(jnp.float32)
        self_rounded = lax.optimization_barrier(self_weight.astype(jnp.bfloat16)).astype(jnp.float32)
        weighted = jnp.einsum("tsh,shd->thd", rounded, values[source_ids])
        weighted = weighted + self_rounded[:, :, None] * values[target_ids]
        heads_out = jax.nn.elu(weighted / denominator[:, :, None]).astype(jnp.bfloat16).reshape(TILE, HEADS * HD)
        return jnp.dot(heads_out, out_weight, preferred_element_type=jnp.float32).astype(jnp.bfloat16)

    return lax.map(one_tile, jnp.arange(TILE_COUNT, dtype=jnp.int32)).reshape(NODES, OUT)
```

```python
import functools

import jax
import jax.numpy as jnp
import numpy as np
from jax import lax
from jax.experimental import pallas as pl
from jax.experimental.pallas import tpu as pltpu
from jax.sharding import Mesh
from jax.sharding import PartitionSpec as P

NODE = ("yh", "z", "x")
HEAD = ("yl", "c")
LOW = -3.0e38


def leaky_relu(values):
    return jnp.maximum(values, 0.2 * values)


def pick_kernel(presence_ref, gathered_ref, out_ref):
    copies = out_ref.shape[0]
    slots = out_ref.shape[1]

    def visit(tile, slot):
        here = presence_ref[0, tile]

        @pl.when((here == 1) & (slot < slots))
        def _():
            rows = gathered_ref[tile]
            for i in range(copies):
                out_ref[i, slot] = rows

        return slot + here

    lax.fori_loop(0, gathered_ref.shape[0], visit, jnp.int32(0))


def attend_kernel(
    where_ref,
    presence_ref,
    own_ref,
    other_ref,
    features_ref,
    proj_ref,
    source_ref,
    target_ref,
    weight_ref,
    masks_hbm,
    out_ref,
    masks,
    values,
    weights,
    sem,
):
    slots, tile, _ = masks.shape
    groups = own_ref.shape[0]
    part = own_ref.shape[2]
    copy = pltpu.make_async_copy(masks_hbm.at[0], masks, sem)
    copy.start()
    node = where_ref[0]
    core = where_ref[1]

    def project(rows):
        return jnp.dot(rows, proj_ref[...], preferred_element_type=jnp.float32).astype(jnp.bfloat16)

    for ref, side in ((own_ref, core), (other_ref, 1 - core)):
        for group in range(groups):
            rows = project(ref[group].reshape(slots * part, tile))
            values[:, group, side] = rows.reshape(slots, part, tile)

    local = project(features_ref[...])
    local_wide = local.astype(jnp.float32)
    target_terms = jnp.sum(local_wide * target_ref[...], axis=1, keepdims=True)
    self_source = jnp.sum(local_wide * source_ref[...], axis=1, keepdims=True)

    source = source_ref[...]
    high = source.astype(jnp.bfloat16).astype(jnp.float32)
    rest = source - high
    middle = rest.astype(jnp.bfloat16).astype(jnp.float32)
    low = rest - middle
    row = lax.broadcasted_iota(jnp.int32, (16, tile), 0)
    split = jnp.where(row == 0, high, jnp.where(row == 1, middle, jnp.where(row == 2, low, 0.0)))
    projected = values[...].reshape(slots * tile, tile)
    terms = lax.dot_general(
        split.astype(jnp.bfloat16),
        projected,
        (((1,), (1,)), ((), ())),
        preferred_element_type=jnp.float32,
    )
    source_terms = terms[0:1] + terms[1:2] + terms[2:3]

    def count(i, rank):
        return rank + presence_ref[0, i]

    rank = lax.fori_loop(0, node, count, jnp.int32(0))
    copy.wait()

    @pl.when(presence_ref[0, node] == 1)
    def _():
        down = lax.broadcasted_iota(jnp.int32, (tile, tile), 0)
        across = lax.broadcasted_iota(jnp.int32, (tile, tile), 1)
        masks[rank] = jnp.where(down == across, 0, masks[rank])

    best = jnp.full((tile, tile), LOW, jnp.float32)
    for k in range(slots):
        terms_here = source_terms[:, k * tile : (k + 1) * tile]
        best = jnp.maximum(best, jnp.where(masks[k] == 1, terms_here, LOW))
    top = jnp.maximum(jnp.max(best, axis=1, keepdims=True), self_source)
    peak = leaky_relu(target_terms + top)
    self_weight = jnp.exp(leaky_relu(target_terms + self_source) - peak)

    total = jnp.zeros((tile, tile), jnp.float32)
    for k in range(slots):
        scores = leaky_relu(target_terms + source_terms[:, k * tile : (k + 1) * tile])
        edge = jnp.where(masks[k] == 1, jnp.exp(scores - peak), 0.0)
        total = total + edge
        weights[:, k * tile : (k + 1) * tile] = edge.astype(jnp.bfloat16)
    denominator = jnp.sum(total, axis=1, keepdims=True) + self_weight
    summed = jnp.dot(weights[...], projected, preferred_element_type=jnp.float32)
    summed = summed + self_weight.astype(jnp.bfloat16).astype(jnp.float32) * local_wide
    attended = summed / denominator
    below = jnp.minimum(attended, 0.0)
    half = jnp.tanh(0.5 * below)
    heads_out = jnp.where(attended > 0, attended, 2.0 * half / (1.0 - half)).astype(jnp.bfloat16)
    out_ref[...] = jnp.dot(
        heads_out, weight_ref[...], preferred_element_type=jnp.float32
    ).astype(jnp.bfloat16)


def per_device(sizes, features, proj_weight, score_source, score_target, out_weight, presence, tile_masks):
    nodes, lows, cores = sizes
    tile, width = features.shape
    slots = tile_masks.shape[1]
    part = tile // (lows * cores)
    vmem = pl.BlockSpec(memory_space=pltpu.VMEM)
    smem = pl.BlockSpec(memory_space=pltpu.SMEM)

    core = lax.axis_index("c")
    first = lax.axis_index(HEAD) * part
    mine = lax.dynamic_slice(features, (first, 0), (part, width))
    gathered = lax.all_to_all(
        jnp.broadcast_to(mine[None], (nodes, part, width)), NODE, 0, 0, tiled=True
    )
    picked = pl.pallas_call(
        pick_kernel,
        out_shape=jax.ShapeDtypeStruct((lows, slots, part, width), jnp.bfloat16),
        in_specs=[smem, vmem],
        out_specs=vmem,
        compiler_params=pltpu.CompilerParams(vmem_limit_bytes=4 << 20),
        name="pick",
    )(presence, gathered)
    own = lax.all_to_all(picked, "yl", 0, 0, tiled=True)
    swap = [(0, 1), (1, 0)]
    other = lax.ppermute(own, "c", swap)
    place = jnp.stack([lax.axis_index(NODE), core]).astype(jnp.int32)
    partial = pl.pallas_call(
        attend_kernel,
        out_shape=jax.ShapeDtypeStruct((tile, out_weight.shape[1]), jnp.bfloat16),
        in_specs=[smem, smem] + [vmem] * 7 + [pl.BlockSpec(memory_space=pl.ANY)],
        out_specs=vmem,
        scratch_shapes=[
            pltpu.VMEM((slots, tile, tile), jnp.int32),
            pltpu.VMEM((slots, lows, cores, part, width), jnp.bfloat16),
            pltpu.VMEM((tile, slots * tile), jnp.bfloat16),
            pltpu.SemaphoreType.DMA,
        ],
        compiler_params=pltpu.CompilerParams(vmem_limit_bytes=16 << 20),
        name="attend",
    )(place, presence, own, other, features, proj_weight, score_source, score_target, out_weight, tile_masks)
    paired = partial.astype(jnp.float32) + lax.ppermute(partial, "c", swap).astype(jnp.float32)
    paired = jnp.broadcast_to(paired.astype(jnp.bfloat16)[None], (lows,) + partial.shape)
    pieces = lax.all_to_all(paired, "yl", 0, 0, tiled=True)
    return jnp.sum(pieces.astype(jnp.float32), axis=0).astype(jnp.bfloat16)


def solution(mesh):
    fine = Mesh(np.asarray(mesh.devices).reshape(2, 8, 4, 4, 2), NODE + HEAD)
    return jax.shard_map(
        functools.partial(per_device, (64, 4, 2)),
        mesh=fine,
        in_specs=(
            P(NODE, None),
            P(None, HEAD),
            P(HEAD, None),
            P(HEAD, None),
            P(HEAD, None),
            P(NODE, None),
            P(NODE, None, None, None),
        ),
        out_specs=P(NODE, None),
        check_vma=False,
    )
```

```python
import functools

import jax
import jax.numpy as jnp
import numpy as np
from jax import lax
from jax.experimental import pallas as pl
from jax.experimental.pallas import tpu as pltpu
from jax.sharding import Mesh
from jax.sharding import PartitionSpec as P

NODE = ("yh", "z", "x")
HEAD = ("yl", "c")
EVERY = NODE + ("yl",)
SIZES = {"yh": 2, "z": 8, "x": 4, "yl": 4, "c": 2}
NODES = 64
QUARTERS = 4
LOW = -1.0e38


def node_groups():
    groups = []
    for pair in range(SIZES["yl"]):
        group = []
        for yh in range(SIZES["yh"]):
            for z in range(SIZES["z"]):
                for x in range(SIZES["x"]):
                    place = (yh * SIZES["z"] + z) * SIZES["x"] + x
                    group.append(place * SIZES["yl"] + (pair ^ (2 * yh)))
        groups.append(group)
    return groups


def leaky_relu(values):
    return jnp.maximum(values, 0.2 * values)


def prepare_kernel(features_hbm, presence_hbm, send_ref, presence_ref, rows_ref, sems):
    part = rows_ref.shape[0]
    start = (lax.rem(lax.axis_index("yl"), 2) * 2 + lax.axis_index("c")) * part
    rows_copy = pltpu.make_async_copy(
        features_hbm.at[pl.ds(pl.multiple_of(start, part), part)], rows_ref, sems.at[0]
    )
    presence_copy = pltpu.make_async_copy(presence_hbm, presence_ref, sems.at[1])
    rows_copy.start()
    presence_copy.start()
    rows_copy.wait()
    rows = rows_ref[...]
    for i in range(send_ref.shape[0]):
        send_ref[i] = rows
    presence_copy.wait()


def pick_kernel(presence_ref, gathered_ref, out_ref, slots_ref):
    slot = jnp.int32(0)
    for tile in range(gathered_ref.shape[0]):
        slots_ref[slot] = gathered_ref[tile]
        slot = jnp.minimum(slot + presence_ref[0, tile], out_ref.shape[0])
    for i in range(out_ref.shape[0]):
        out_ref[i] = slots_ref[i]


def attend_kernel(
    presence_ref,
    own_ref,
    beside_ref,
    twin_ref,
    across_ref,
    features_ref,
    proj_ref,
    source_ref,
    target_ref,
    weight_ref,
    masks_ref,
    out_ref,
    values,
    masked,
    weights,
):
    slots, tile, _ = masked.shape
    part = own_ref.shape[1]
    node = (lax.axis_index("yh") * SIZES["z"] + lax.axis_index("z")) * SIZES["x"] + lax.axis_index("x")
    half = lax.rem(lax.axis_index("yl"), 2)
    core = lax.axis_index("c")

    def project(rows):
        return jnp.dot(rows, proj_ref[...], preferred_element_type=jnp.float32).astype(jnp.bfloat16)

    for ref, place, side in (
        (own_ref, half, core),
        (beside_ref, 1 - half, core),
        (twin_ref, half, 1 - core),
        (across_ref, 1 - half, 1 - core),
    ):
        rows = project(ref[...].reshape(slots * part, tile))
        values[:, place, side] = rows.reshape(slots, part, tile)

    local = project(features_ref[...])
    local_wide = local.astype(jnp.float32)
    target_terms = jnp.sum(local_wide * target_ref[...], axis=1, keepdims=True)
    self_source = jnp.sum(local_wide * source_ref[...], axis=1, keepdims=True)

    source = source_ref[...]
    high = source.astype(jnp.bfloat16).astype(jnp.float32)
    rest = source - high
    middle = rest.astype(jnp.bfloat16).astype(jnp.float32)
    low = rest - middle
    row = lax.broadcasted_iota(jnp.int32, (16, tile), 0)
    split = jnp.where(row == 0, high, jnp.where(row == 1, middle, jnp.where(row == 2, low, 0.0)))
    projected = values[...].reshape(slots * tile, tile)
    terms = lax.dot_general(
        split.astype(jnp.bfloat16),
        projected,
        (((1,), (1,)), ((), ())),
        preferred_element_type=jnp.float32,
    )
    source_terms = terms[0:1] + terms[1:2] + terms[2:3]

    best = jnp.full((tile, tile), LOW, jnp.float32)
    for k in range(slots):
        terms_here = source_terms[:, k * tile : (k + 1) * tile]
        linked = jnp.where(masks_ref[0, k] == 1, terms_here, LOW)
        masked[k] = linked
        best = jnp.maximum(best, linked)
    top = jnp.maximum(jnp.max(best, axis=1, keepdims=True), self_source)
    peak = leaky_relu(target_terms + top)
    self_weight = jnp.exp(leaky_relu(target_terms + self_source) - peak)

    def count(i, rank):
        return rank + presence_ref[0, i]

    rank = lax.fori_loop(0, node, count, jnp.int32(0))

    @pl.when(presence_ref[0, node] == 1)
    def _():
        down = lax.broadcasted_iota(jnp.int32, (tile, tile), 0)
        over = lax.broadcasted_iota(jnp.int32, (tile, tile), 1)
        masked[rank] = jnp.where(down == over, LOW, masked[rank])

    total = jnp.zeros((tile, tile), jnp.float32)
    for k in range(slots):
        edge = jnp.exp(leaky_relu(target_terms + masked[k]) - peak)
        total = total + edge
        weights[:, k * tile : (k + 1) * tile] = edge.astype(jnp.bfloat16)
    denominator = jnp.sum(total, axis=1, keepdims=True) + self_weight
    summed = jnp.dot(weights[...], projected, preferred_element_type=jnp.float32)
    summed = summed + self_weight.astype(jnp.bfloat16).astype(jnp.float32) * local_wide
    attended = summed / denominator
    below = jnp.minimum(attended, 0.0)
    bent = jnp.tanh(0.5 * below)
    heads_out = jnp.where(attended > 0, attended, 2.0 * bent / (1.0 - bent)).astype(jnp.bfloat16)
    out_ref[...] = jnp.dot(
        heads_out, weight_ref[...], preferred_element_type=jnp.float32
    ).astype(jnp.bfloat16)


def per_device(features, proj_weight, score_source, score_target, out_weight, presence, tile_masks):
    tile, width = features.shape
    slots = tile_masks.shape[1]
    part = tile // QUARTERS
    vmem = pl.BlockSpec(memory_space=pltpu.VMEM)
    smem = pl.BlockSpec(memory_space=pltpu.SMEM)
    raw = pl.BlockSpec(memory_space=pltpu.HBM)

    send, presence = pl.pallas_call(
        prepare_kernel,
        out_shape=(
            jax.ShapeDtypeStruct((NODES, part, width), jnp.bfloat16),
            jax.ShapeDtypeStruct(presence.shape, jnp.int32),
        ),
        in_specs=[raw, raw],
        out_specs=(vmem, vmem),
        scratch_shapes=[pltpu.VMEM((part, width), jnp.bfloat16), pltpu.SemaphoreType.DMA((2,))],
        compiler_params=pltpu.CompilerParams(vmem_limit_bytes=4 << 20),
        name="prepare",
    )(features, presence)
    gathered = lax.all_to_all(
        send, EVERY, 0, 0, tiled=True, axis_index_groups=node_groups()
    )
    own = pl.pallas_call(
        pick_kernel,
        out_shape=jax.ShapeDtypeStruct((slots, part, width), jnp.bfloat16),
        in_specs=[smem, vmem],
        out_specs=vmem,
        scratch_shapes=[pltpu.VMEM((slots + 1, part, width), jnp.bfloat16)],
        compiler_params=pltpu.CompilerParams(vmem_limit_bytes=4 << 20),
        name="pick",
    )(presence, gathered)
    swap = [(0, 1), (1, 0)]
    beside = lax.ppermute(own, "yl", [(i, i ^ 1) for i in range(SIZES["yl"])])
    twin = lax.ppermute(own, "c", swap)
    across = lax.ppermute(beside, "c", swap)
    partial = pl.pallas_call(
        attend_kernel,
        out_shape=jax.ShapeDtypeStruct((tile, out_weight.shape[1]), jnp.bfloat16),
        in_specs=[smem] + [vmem] * 10,
        out_specs=vmem,
        scratch_shapes=[
            pltpu.VMEM((slots, 2, 2, part, width), jnp.bfloat16),
            pltpu.VMEM((slots, tile, tile), jnp.float32),
            pltpu.VMEM((tile, slots * tile), jnp.bfloat16),
        ],
        compiler_params=pltpu.CompilerParams(vmem_limit_bytes=16 << 20),
        name="attend",
    )(
        presence, own, beside, twin, across, features,
        proj_weight, score_source, score_target, out_weight, tile_masks,
    )
    paired = partial.astype(jnp.float32) + lax.ppermute(partial, "c", swap).astype(jnp.float32)
    lows = SIZES["yl"]
    paired = jnp.broadcast_to(paired.astype(jnp.bfloat16)[None], (lows,) + partial.shape)
    pieces = lax.all_to_all(paired, "yl", 0, 0, tiled=True)
    return jnp.sum(pieces.astype(jnp.float32), axis=0).astype(jnp.bfloat16)


def solution(mesh):
    shape = tuple(SIZES[name] for name in NODE + HEAD)
    fine = Mesh(np.asarray(mesh.devices).reshape(shape), NODE + HEAD)
    return jax.shard_map(
        per_device,
        mesh=fine,
        in_specs=(
            P(NODE, None),
            P(None, HEAD),
            P(HEAD, None),
            P(HEAD, None),
            P(HEAD, None),
            P(NODE, None),
            P(NODE, None, None, None),
        ),
        out_specs=P(NODE, None),
        check_vma=False,
    )
```

```python
import functools

import jax
import jax.numpy as jnp
import numpy as np
from jax import lax
from jax.experimental import pallas as pl
from jax.experimental.pallas import tpu as pltpu
from jax.sharding import Mesh
from jax.sharding import PartitionSpec as P

NODE = ("yh", "z", "x")
HEAD = ("yl", "c")
EVERY = NODE + ("yl",)
SIZES = {"yh": 2, "z": 8, "x": 4, "yl": 4, "c": 2}
NODES = 64
EIGHTHS = 8
LOW = -1.0e38


def node_groups():
    groups = []
    for pair in range(SIZES["yl"]):
        group = []
        for yh in range(SIZES["yh"]):
            for z in range(SIZES["z"]):
                for x in range(SIZES["x"]):
                    place = (yh * SIZES["z"] + z) * SIZES["x"] + x
                    group.append(place * SIZES["yl"] + (pair ^ (2 * yh)))
        groups.append(group)
    return groups


def pair_of_device():
    return lax.axis_index("yl") ^ (2 * lax.axis_index("yh"))


def toward(flip):
    return [(i, i ^ flip) for i in range(SIZES["yl"])]


def leaky_relu(values):
    return jnp.maximum(values, 0.2 * values)


def prepare_kernel(features_hbm, presence_hbm, send_ref, presence_ref, rows_ref, sems):
    part = rows_ref.shape[0]
    start = (pair_of_device() * SIZES["c"] + lax.axis_index("c")) * part
    rows_copy = pltpu.make_async_copy(
        features_hbm.at[pl.ds(pl.multiple_of(start, part), part)], rows_ref, sems.at[0]
    )
    presence_copy = pltpu.make_async_copy(presence_hbm, presence_ref, sems.at[1])
    rows_copy.start()
    presence_copy.start()
    rows_copy.wait()
    rows = rows_ref[...]
    for i in range(send_ref.shape[0]):
        send_ref[i] = rows
    presence_copy.wait()


def pick_kernel(presence_ref, gathered_ref, out_ref, slots_ref):
    slot = jnp.int32(0)
    for tile in range(gathered_ref.shape[0]):
        slots_ref[slot] = gathered_ref[tile]
        slot = jnp.minimum(slot + presence_ref[0, tile], out_ref.shape[0])
    for i in range(out_ref.shape[0]):
        out_ref[i] = slots_ref[i]


def attend_kernel(
    presence_ref,
    first_ref,
    second_ref,
    other_ref,
    features_ref,
    proj_ref,
    source_ref,
    target_ref,
    weight_ref,
    masks_ref,
    out_ref,
    values,
    masked,
    weights,
):
    slots, tile, _ = masked.shape
    part = first_ref.shape[2]
    node = (lax.axis_index("yh") * SIZES["z"] + lax.axis_index("z")) * SIZES["x"] + lax.axis_index("x")
    pair = pair_of_device()
    core = lax.axis_index("c")

    def project(rows):
        return jnp.dot(rows, proj_ref[...], preferred_element_type=jnp.float32).astype(jnp.bfloat16)

    for i, flip in enumerate((0, 2, 1, 3)):
        mine = (first_ref if i < 2 else second_ref)[i % 2]
        for rows, side in ((mine, core), (other_ref[i], 1 - core)):
            rows = project(rows.reshape(slots * part, tile))
            values[:, pair ^ flip, side] = rows.reshape(slots, part, tile)

    local = project(features_ref[...])
    local_wide = local.astype(jnp.float32)
    target_terms = jnp.sum(local_wide * target_ref[...], axis=1, keepdims=True)
    self_source = jnp.sum(local_wide * source_ref[...], axis=1, keepdims=True)

    source = source_ref[...]
    high = source.astype(jnp.bfloat16).astype(jnp.float32)
    rest = source - high
    middle = rest.astype(jnp.bfloat16).astype(jnp.float32)
    low = rest - middle
    row = lax.broadcasted_iota(jnp.int32, (16, tile), 0)
    split = jnp.where(row == 0, high, jnp.where(row == 1, middle, jnp.where(row == 2, low, 0.0)))
    projected = values[...].reshape(slots * tile, tile)
    terms = lax.dot_general(
        split.astype(jnp.bfloat16),
        projected,
        (((1,), (1,)), ((), ())),
        preferred_element_type=jnp.float32,
    )
    source_terms = terms[0:1] + terms[1:2] + terms[2:3]

    best = jnp.full((tile, tile), LOW, jnp.float32)
    for k in range(slots):
        terms_here = source_terms[:, k * tile : (k + 1) * tile]
        linked = jnp.where(masks_ref[0, k] == 1, terms_here, LOW)
        masked[k] = linked
        best = jnp.maximum(best, linked)
    top = jnp.maximum(jnp.max(best, axis=1, keepdims=True), self_source)
    peak = leaky_relu(target_terms + top)
    self_weight = jnp.exp(leaky_relu(target_terms + self_source) - peak)

    def count(i, rank):
        return rank + presence_ref[0, i]

    rank = lax.fori_loop(0, node, count, jnp.int32(0))

    @pl.when(presence_ref[0, node] == 1)
    def _():
        down = lax.broadcasted_iota(jnp.int32, (tile, tile), 0)
        over = lax.broadcasted_iota(jnp.int32, (tile, tile), 1)
        masked[rank] = jnp.where(down == over, LOW, masked[rank])

    total = jnp.zeros((tile, tile), jnp.float32)
    for k in range(slots):
        edge = jnp.exp(leaky_relu(target_terms + masked[k]) - peak)
        total = total + edge
        weights[:, k * tile : (k + 1) * tile] = edge.astype(jnp.bfloat16)
    denominator = jnp.sum(total, axis=1, keepdims=True) + self_weight
    summed = jnp.dot(weights[...], projected, preferred_element_type=jnp.float32)
    summed = summed + self_weight.astype(jnp.bfloat16).astype(jnp.float32) * local_wide
    attended = summed / denominator
    below = jnp.minimum(attended, 0.0)
    bent = jnp.tanh(0.5 * below)
    heads_out = jnp.where(attended > 0, attended, 2.0 * bent / (1.0 - bent)).astype(jnp.bfloat16)
    out_ref[...] = jnp.dot(
        heads_out, weight_ref[...], preferred_element_type=jnp.float32
    ).astype(jnp.bfloat16)


def per_device(features, proj_weight, score_source, score_target, out_weight, presence, tile_masks):
    tile, width = features.shape
    slots = tile_masks.shape[1]
    part = tile // EIGHTHS
    vmem = pl.BlockSpec(memory_space=pltpu.VMEM)
    smem = pl.BlockSpec(memory_space=pltpu.SMEM)
    raw = pl.BlockSpec(memory_space=pltpu.HBM)

    features_far = pltpu.with_memory_space_constraint(features, pltpu.HBM)
    presence_far = pltpu.with_memory_space_constraint(presence, pltpu.HBM)
    send, presence = pl.pallas_call(
        prepare_kernel,
        out_shape=(
            jax.ShapeDtypeStruct((NODES, part, width), jnp.bfloat16),
            jax.ShapeDtypeStruct(presence.shape, jnp.int32),
        ),
        in_specs=[raw, raw],
        out_specs=(vmem, vmem),
        scratch_shapes=[pltpu.VMEM((part, width), jnp.bfloat16), pltpu.SemaphoreType.DMA((2,))],
        compiler_params=pltpu.CompilerParams(vmem_limit_bytes=4 << 20),
        name="prepare",
    )(features_far, presence_far)
    gathered = lax.all_to_all(
        send, EVERY, 0, 0, tiled=True, axis_index_groups=node_groups()
    )
    own = pl.pallas_call(
        pick_kernel,
        out_shape=jax.ShapeDtypeStruct((slots, part, width), jnp.bfloat16),
        in_specs=[smem, vmem],
        out_specs=vmem,
        scratch_shapes=[pltpu.VMEM((slots + 1, part, width), jnp.bfloat16)],
        compiler_params=pltpu.CompilerParams(vmem_limit_bytes=4 << 20),
        name="pick",
    )(presence, gathered)
    swap = [(0, 1), (1, 0)]
    first = jnp.stack([own, lax.ppermute(own, "yl", toward(2))])
    second = lax.ppermute(first, "yl", toward(1))
    other = lax.ppermute(jnp.concatenate([first, second]), "c", swap)
    partial = pl.pallas_call(
        attend_kernel,
        out_shape=jax.ShapeDtypeStruct((tile, out_weight.shape[1]), jnp.bfloat16),
        in_specs=[smem] + [vmem] * 9,
        out_specs=vmem,
        scratch_shapes=[
            pltpu.VMEM((slots, SIZES["yl"], SIZES["c"], part, width), jnp.bfloat16),
            pltpu.VMEM((slots, tile, tile), jnp.float32),
            pltpu.VMEM((tile, slots * tile), jnp.bfloat16),
        ],
        compiler_params=pltpu.CompilerParams(vmem_limit_bytes=16 << 20),
        name="attend",
    )(
        presence, first, second, other, features,
        proj_weight, score_source, score_target, out_weight, tile_masks,
    )
    for axis, perm in (("c", swap), ("yl", toward(1)), ("yl", toward(2))):
        moved = lax.ppermute(partial, axis, perm)
        partial = (partial.astype(jnp.float32) + moved.astype(jnp.float32)).astype(jnp.bfloat16)
    return partial


def solution(mesh):
    shape = tuple(SIZES[name] for name in NODE + HEAD)
    fine = Mesh(np.asarray(mesh.devices).reshape(shape), NODE + HEAD)
    return jax.shard_map(
        per_device,
        mesh=fine,
        in_specs=(
            P(NODE, None),
            P(None, HEAD),
            P(HEAD, None),
            P(HEAD, None),
            P(HEAD, None),
            P(NODE, None),
            P(NODE, None, None, None),
        ),
        out_specs=P(NODE, None),
        check_vma=False,
    )
```

```python
import functools

import jax
import jax.numpy as jnp
import numpy as np
from jax import lax
from jax.experimental import pallas as pl
from jax.experimental.pallas import tpu as pltpu
from jax.sharding import Mesh
from jax.sharding import PartitionSpec as P

NODE = ("yh", "z", "x")
HEAD = ("yl", "c")
EVERY = NODE + ("yl",)
SIZES = {"yh": 2, "z": 8, "x": 4, "yl": 4, "c": 2}
NODES = 64
EIGHTHS = 8
LOW = -1.0e38


def node_groups():
    groups = []
    for pair in range(SIZES["yl"]):
        group = []
        for yh in range(SIZES["yh"]):
            for z in range(SIZES["z"]):
                for x in range(SIZES["x"]):
                    place = (yh * SIZES["z"] + z) * SIZES["x"] + x
                    group.append(place * SIZES["yl"] + (pair ^ (2 * yh)))
        groups.append(group)
    return groups


def pair_of_device():
    return lax.axis_index("yl") ^ (2 * lax.axis_index("yh"))


def leaky_relu(values):
    return jnp.maximum(values, 0.2 * values)


def prepare_kernel(features_hbm, presence_hbm, send_ref, presence_ref, rows_ref, sems):
    part = rows_ref.shape[0]
    start = (pair_of_device() * SIZES["c"] + lax.axis_index("c")) * part
    rows_copy = pltpu.make_async_copy(
        features_hbm.at[pl.ds(pl.multiple_of(start, part), part)], rows_ref, sems.at[0]
    )
    presence_copy = pltpu.make_async_copy(presence_hbm, presence_ref, sems.at[1])
    rows_copy.start()
    presence_copy.start()
    rows_copy.wait()
    rows = rows_ref[...]
    for i in range(send_ref.shape[0]):
        send_ref[i] = rows
    presence_copy.wait()


def pick_kernel(presence_ref, gathered_ref, out_ref, slots_ref):
    slot = jnp.int32(0)
    for tile in range(gathered_ref.shape[0]):
        slots_ref[slot] = gathered_ref[tile]
        slot = jnp.minimum(slot + presence_ref[0, tile], out_ref.shape[1])
    for i in range(out_ref.shape[1]):
        rows = slots_ref[i]
        for copy in range(out_ref.shape[0]):
            out_ref[copy, i] = rows


def split_rows(vector):
    high = vector.astype(jnp.bfloat16).astype(jnp.float32)
    rest = vector - high
    middle = rest.astype(jnp.bfloat16).astype(jnp.float32)
    return high, middle, rest - middle


def pack_kernel(own_ref, proj_ref, weight_ref, source_ref, target_ref, out_ref):
    lows, slots, part, width = own_ref.shape
    rows = lows * slots * part
    out_ref[:rows] = own_ref[...].reshape(rows, width)
    out_ref[rows : rows + width] = proj_ref[...]
    for i in range(weight_ref.shape[1] // width):
        start = rows + (i + 1) * width
        out_ref[start : start + width] = weight_ref[:, i * width : (i + 1) * width]
    row = lax.broadcasted_iota(jnp.int32, (16, width), 0)
    block = jnp.zeros((16, width), jnp.float32)
    for i, vector in enumerate(split_rows(source_ref[...]) + split_rows(target_ref[...])):
        block = jnp.where(row == i, vector, block)
    out_ref[rows + 3 * width :] = block.astype(jnp.bfloat16)


def attend_kernel(
    presence_ref,
    own_ref,
    other_ref,
    features_ref,
    masks_ref,
    out_ref,
    sources,
    tables,
    masked,
    weights,
):
    slots, lows, cores, part, width = sources.shape
    heads = cores
    tile = masks_ref.shape[2]
    rows = lows * slots * part
    node = (lax.axis_index("yh") * SIZES["z"] + lax.axis_index("z")) * SIZES["x"] + lax.axis_index("x")
    core = lax.axis_index("c")
    for ref, side in ((own_ref, core), (other_ref, 1 - core)):
        tables[side] = ref[rows:]
        for low in range(lows):
            pair = low ^ (2 * lax.axis_index("yh"))
            start = low * slots * part
            sources[:, pair, side] = ref[start : start + slots * part].reshape(slots, part, width)

    both = jnp.concatenate([tables[h, :width] for h in range(heads)], axis=1)

    def project(values):
        return jnp.dot(values, both, preferred_element_type=jnp.float32).astype(jnp.bfloat16)

    projected = project(sources[...].reshape(slots * tile, width))
    local = project(features_ref[...]).astype(jnp.float32)
    vectors = [tables[h, 3 * width :] for h in range(heads)]
    row = lax.broadcasted_iota(jnp.int32, (16, width), 0)

    target_terms, self_source, source_terms = [], [], []
    for h in range(heads):
        wide = vectors[h].astype(jnp.float32)
        source = wide[0:1] + wide[1:2] + wide[2:3]
        target = wide[3:4] + wide[4:5] + wide[5:6]
        mine = local[:, h * width : (h + 1) * width]
        target_terms.append(jnp.sum(mine * target, axis=1, keepdims=True))
        self_source.append(jnp.sum(mine * source, axis=1, keepdims=True))
        terms = lax.dot_general(
            vectors[h],
            projected[:, h * width : (h + 1) * width],
            (((1,), (1,)), ((), ())),
            preferred_element_type=jnp.float32,
        )
        source_terms.append(terms[0:1] + terms[1:2] + terms[2:3])

    best = [jnp.full((tile, tile), LOW, jnp.float32) for h in range(heads)]
    for k in range(slots):
        linked = masks_ref[0, k] == 1
        for h in range(heads):
            value = jnp.where(linked, source_terms[h][:, k * tile : (k + 1) * tile], LOW)
            masked[h, k] = value
            best[h] = jnp.maximum(best[h], value)

    def count(i, rank):
        return rank + presence_ref[0, i]

    rank = lax.fori_loop(0, node, count, jnp.int32(0))

    @pl.when(presence_ref[0, node] == 1)
    def _():
        down = lax.broadcasted_iota(jnp.int32, (tile, tile), 0)
        over = lax.broadcasted_iota(jnp.int32, (tile, tile), 1)
        for h in range(heads):
            masked[h, rank] = jnp.where(down == over, LOW, masked[h, rank])

    outs = []
    for h in range(heads):
        mine = local[:, h * width : (h + 1) * width]
        top = jnp.maximum(jnp.max(best[h], axis=1, keepdims=True), self_source[h])
        peak = leaky_relu(target_terms[h] + top)
        self_weight = jnp.exp(leaky_relu(target_terms[h] + self_source[h]) - peak)
        total = jnp.zeros((tile, tile), jnp.float32)
        for k in range(slots):
            edge = jnp.exp(leaky_relu(target_terms[h] + masked[h, k]) - peak)
            total = total + edge
            weights[h, :, k * tile : (k + 1) * tile] = edge.astype(jnp.bfloat16)
        denominator = jnp.sum(total, axis=1, keepdims=True) + self_weight
        summed = jnp.dot(
            weights[h],
            projected[:, h * width : (h + 1) * width],
            preferred_element_type=jnp.float32,
        )
        summed = summed + self_weight.astype(jnp.bfloat16).astype(jnp.float32) * mine
        attended = summed / denominator
        below = jnp.minimum(attended, 0.0)
        bent = jnp.tanh(0.5 * below)
        outs.append(jnp.where(attended > 0, attended, 2.0 * bent / (1.0 - bent)).astype(jnp.bfloat16))
    joined = jnp.concatenate(outs, axis=1)
    columns = []
    for i in (1, 2):
        table = jnp.concatenate(
            [tables[h, i * width : (i + 1) * width] for h in range(heads)], axis=0
        )
        columns.append(jnp.dot(joined, table, preferred_element_type=jnp.float32))
    mixed = jnp.concatenate(columns, axis=1).astype(jnp.bfloat16)
    for copy in range(out_ref.shape[0]):
        out_ref[copy] = mixed


def per_device(features, proj_weight, score_source, score_target, out_weight, presence, tile_masks):
    tile, width = features.shape
    slots = tile_masks.shape[1]
    part = tile // EIGHTHS
    lows = SIZES["yl"]
    vmem = pl.BlockSpec(memory_space=pltpu.VMEM)
    smem = pl.BlockSpec(memory_space=pltpu.SMEM)
    raw = pl.BlockSpec(memory_space=pltpu.HBM)

    features_far = pltpu.with_memory_space_constraint(features, pltpu.HBM)
    presence_far = pltpu.with_memory_space_constraint(presence, pltpu.HBM)
    send, presence = pl.pallas_call(
        prepare_kernel,
        out_shape=(
            jax.ShapeDtypeStruct((NODES, part, width), jnp.bfloat16),
            jax.ShapeDtypeStruct(presence.shape, jnp.int32),
        ),
        in_specs=[raw, raw],
        out_specs=(vmem, vmem),
        scratch_shapes=[pltpu.VMEM((part, width), jnp.bfloat16), pltpu.SemaphoreType.DMA((2,))],
        compiler_params=pltpu.CompilerParams(vmem_limit_bytes=4 << 20),
        name="prepare",
    )(features_far, presence_far)
    gathered = lax.all_to_all(
        send, EVERY, 0, 0, tiled=True, axis_index_groups=node_groups()
    )
    picked = pl.pallas_call(
        pick_kernel,
        out_shape=jax.ShapeDtypeStruct((lows, slots, part, width), jnp.bfloat16),
        in_specs=[smem, vmem],
        out_specs=vmem,
        scratch_shapes=[pltpu.VMEM((slots + 1, part, width), jnp.bfloat16)],
        compiler_params=pltpu.CompilerParams(vmem_limit_bytes=4 << 20),
        name="pick",
    )(presence, gathered)
    swap = [(0, 1), (1, 0)]
    own = lax.all_to_all(picked, "yl", 0, 0, tiled=True)
    payload = lows * slots * part + 3 * width + 16
    packed = pl.pallas_call(
        pack_kernel,
        out_shape=jax.ShapeDtypeStruct((payload, width), jnp.bfloat16),
        in_specs=[vmem] * 5,
        out_specs=vmem,
        compiler_params=pltpu.CompilerParams(vmem_limit_bytes=4 << 20),
        name="pack",
    )(own, proj_weight, out_weight, score_source, score_target)
    other = lax.ppermute(packed, "c", swap)
    cores = SIZES["c"]
    paired = pl.pallas_call(
        attend_kernel,
        out_shape=jax.ShapeDtypeStruct((lows, tile, out_weight.shape[1]), jnp.bfloat16),
        in_specs=[smem] + [vmem] * 4,
        out_specs=vmem,
        scratch_shapes=[
            pltpu.VMEM((slots, lows, cores, part, width), jnp.bfloat16),
            pltpu.VMEM((cores, 3 * width + 16, width), jnp.bfloat16),
            pltpu.VMEM((cores, slots, tile, tile), jnp.float32),
            pltpu.VMEM((cores, tile, slots * tile), jnp.bfloat16),
        ],
        compiler_params=pltpu.CompilerParams(vmem_limit_bytes=16 << 20),
        name="attend",
    )(presence, packed, other, features, tile_masks)
    pieces = lax.all_to_all(paired, "yl", 0, 0, tiled=True)
    return jnp.sum(pieces.astype(jnp.float32), axis=0).astype(jnp.bfloat16)


def solution(mesh):
    shape = tuple(SIZES[name] for name in NODE + HEAD)
    fine = Mesh(np.asarray(mesh.devices).reshape(shape), NODE + HEAD)
    return jax.shard_map(
        per_device,
        mesh=fine,
        in_specs=(
            P(NODE, None),
            P(None, HEAD),
            P(HEAD, None),
            P(HEAD, None),
            P(HEAD, None),
            P(NODE, None),
            P(NODE, None, None, None),
        ),
        out_specs=P(NODE, None),
        check_vma=False,
    )
```

```python
import functools

import jax
import jax.numpy as jnp
import numpy as np
from jax import lax
from jax.experimental import pallas as pl
from jax.experimental.pallas import tpu as pltpu
from jax.sharding import Mesh
from jax.sharding import PartitionSpec as P

NODE = ("yh", "z", "x")
HEAD = ("yl", "c")
EVERY = NODE + ("yl",)
SIZES = {"yh": 2, "z": 8, "x": 4, "yl": 4, "c": 2}
NODES = 64
EIGHTHS = 8
LOW = -1.0e38
LOG2E = 1.4426950408889634


def node_groups():
    groups = []
    for pair in range(SIZES["yl"]):
        group = []
        for yh in range(SIZES["yh"]):
            for z in range(SIZES["z"]):
                for x in range(SIZES["x"]):
                    place = (yh * SIZES["z"] + z) * SIZES["x"] + x
                    group.append(place * SIZES["yl"] + (pair ^ (2 * yh)))
        groups.append(group)
    return groups


def pair_of_device():
    return lax.axis_index("yl") ^ (2 * lax.axis_index("yh"))


def leaky_relu(values):
    return jnp.maximum(values, 0.2 * values)


def prepare_kernel(features_hbm, presence_hbm, send_ref, presence_ref, rows_ref, sems):
    part = rows_ref.shape[0]
    start = (pair_of_device() * SIZES["c"] + lax.axis_index("c")) * part
    rows_copy = pltpu.make_async_copy(
        features_hbm.at[pl.ds(pl.multiple_of(start, part), part)], rows_ref, sems.at[0]
    )
    presence_copy = pltpu.make_async_copy(presence_hbm, presence_ref, sems.at[1])
    rows_copy.start()
    presence_copy.start()
    rows_copy.wait()
    rows = rows_ref[...]
    for i in range(send_ref.shape[0]):
        send_ref[i] = rows
    presence_copy.wait()


def pick_kernel(presence_ref, gathered_ref, out_ref, slots_ref):
    slot = jnp.int32(0)
    for tile in range(gathered_ref.shape[0]):
        slots_ref[slot] = gathered_ref[tile]
        slot = jnp.minimum(slot + presence_ref[0, tile], out_ref.shape[1])
    for i in range(out_ref.shape[1]):
        rows = slots_ref[i]
        for copy in range(out_ref.shape[0]):
            out_ref[copy, i] = rows


def split_rows(vector):
    high = vector.astype(jnp.bfloat16).astype(jnp.float32)
    rest = vector - high
    middle = rest.astype(jnp.bfloat16).astype(jnp.float32)
    return high, middle, rest - middle


def pack_kernel(own_ref, proj_ref, weight_ref, source_ref, target_ref, out_ref):
    lows, slots, part, width = own_ref.shape
    rows = lows * slots * part
    out_ref[:rows] = own_ref[...].reshape(rows, width)
    out_ref[rows : rows + width] = proj_ref[...]
    for i in range(weight_ref.shape[1] // width):
        start = rows + (i + 1) * width
        out_ref[start : start + width] = weight_ref[:, i * width : (i + 1) * width]
    row = lax.broadcasted_iota(jnp.int32, (16, width), 0)
    block = jnp.zeros((16, width), jnp.float32)
    for i, vector in enumerate(split_rows(source_ref[...]) + split_rows(target_ref[...])):
        block = jnp.where(row == i, vector, block)
    out_ref[rows + 3 * width :] = block.astype(jnp.bfloat16)


def mask_kernel(presence_ref, masks_ref, out_ref):
    _, slots, tile, _ = masks_ref.shape
    node = (lax.axis_index("yh") * SIZES["z"] + lax.axis_index("z")) * SIZES["x"] + lax.axis_index("x")
    for k in range(slots):
        out_ref[k] = jnp.where(masks_ref[0, k] == 1, 0.0, LOW)

    def count(i, rank):
        return rank + presence_ref[0, i]

    rank = lax.fori_loop(0, node, count, jnp.int32(0))

    @pl.when(presence_ref[0, node] == 1)
    def _():
        down = lax.broadcasted_iota(jnp.int32, (tile, tile), 0)
        over = lax.broadcasted_iota(jnp.int32, (tile, tile), 1)
        out_ref[rank] = jnp.where(down == over, LOW, out_ref[rank])


def attend_kernel(own_ref, other_ref, features_ref, added_ref, out_ref, values, tables):
    slots, lows, cores, part, columns = values.shape
    heads = cores
    width = columns // heads
    tile = added_ref.shape[1]
    share = slots * part
    rows = lows * share
    core = lax.axis_index("c")
    for ref, side in ((own_ref, core), (other_ref, 1 - core)):
        tables[side] = ref[rows:]
    both = jnp.concatenate([tables[h, :width] for h in range(heads)], axis=1)

    def project(block):
        return jnp.dot(block, both, preferred_element_type=jnp.float32).astype(jnp.bfloat16)

    for ref, side in ((own_ref, core), (other_ref, 1 - core)):
        for low in range(lows):
            pair = low ^ (2 * lax.axis_index("yh"))
            block = project(ref[low * share : (low + 1) * share])
            values[:, pair, side] = block.reshape(slots, part, columns)

    local = project(features_ref[...]).astype(jnp.float32)
    row = lax.broadcasted_iota(jnp.int32, (16, width), 0)
    target_terms, self_source, spread = [], [], []
    for h in range(heads):
        wide = tables[h, 3 * width :].astype(jnp.float32)
        source = wide[0:1] + wide[1:2] + wide[2:3]
        target = wide[3:4] + wide[4:5] + wide[5:6]
        mine = local[:, h * width : (h + 1) * width]
        target_terms.append(LOG2E * jnp.sum(mine * target, axis=1, keepdims=True))
        self_source.append(LOG2E * jnp.sum(mine * source, axis=1, keepdims=True))
        block = jnp.zeros((16, width), jnp.float32)
        for i in range(3):
            block = jnp.where(row == 8 * h + i, wide[i : i + 1], block)
        spread.append(block)
    terms = lax.dot_general(
        jnp.concatenate(spread, axis=1).astype(jnp.bfloat16),
        values[...].reshape(slots * tile, columns),
        (((1,), (1,)), ((), ())),
        preferred_element_type=jnp.float32,
    )
    source_terms = [
        LOG2E * (terms[8 * h : 8 * h + 1] + terms[8 * h + 1 : 8 * h + 2] + terms[8 * h + 2 : 8 * h + 3])
        for h in range(heads)
    ]

    best = [jnp.full((tile, tile), LOW, jnp.float32) for h in range(heads)]
    for k in range(slots):
        added = added_ref[k]
        for h in range(heads):
            best[h] = jnp.maximum(best[h], source_terms[h][:, k * tile : (k + 1) * tile] + added)
    peaks, self_weights = [], []
    for h in range(heads):
        top = jnp.maximum(jnp.max(best[h], axis=1, keepdims=True), self_source[h])
        peaks.append(leaky_relu(target_terms[h] + top))
        self_weights.append(jnp.exp2(leaky_relu(target_terms[h] + self_source[h]) - peaks[h]))

    totals = [jnp.zeros((tile, tile), jnp.float32) for h in range(heads)]
    sums = [jnp.zeros((tile, width), jnp.float32) for h in range(heads)]
    group = 2
    for first in range(0, slots, group):
        for h in range(heads):
            edges = []
            for k in range(first, first + group):
                scores = source_terms[h][:, k * tile : (k + 1) * tile] + added_ref[k]
                edge = jnp.exp2(leaky_relu(target_terms[h] + scores) - peaks[h])
                totals[h] = totals[h] + edge
                edges.append(edge.astype(jnp.bfloat16))
            near = values[first : first + group, :, :, :, h * width : (h + 1) * width]
            sums[h] = sums[h] + jnp.dot(
                jnp.concatenate(edges, axis=1),
                near.reshape(group * tile, width),
                preferred_element_type=jnp.float32,
            )

    outs = []
    for h in range(heads):
        mine = local[:, h * width : (h + 1) * width]
        denominator = jnp.sum(totals[h], axis=1, keepdims=True) + self_weights[h]
        summed = sums[h] + self_weights[h].astype(jnp.bfloat16).astype(jnp.float32) * mine
        attended = summed / denominator
        below = jnp.minimum(attended, 0.0)
        bent = jnp.tanh(0.5 * below)
        outs.append(jnp.where(attended > 0, attended, 2.0 * bent / (1.0 - bent)).astype(jnp.bfloat16))
    joined = jnp.concatenate(outs, axis=1)
    columns = []
    for i in (1, 2):
        table = jnp.concatenate(
            [tables[h, i * width : (i + 1) * width] for h in range(heads)], axis=0
        )
        columns.append(jnp.dot(joined, table, preferred_element_type=jnp.float32))
    mixed = jnp.concatenate(columns, axis=1).astype(jnp.bfloat16)
    for copy in range(out_ref.shape[0]):
        out_ref[copy] = mixed


def per_device(features, proj_weight, score_source, score_target, out_weight, presence, tile_masks):
    tile, width = features.shape
    slots = tile_masks.shape[1]
    part = tile // EIGHTHS
    lows = SIZES["yl"]
    vmem = pl.BlockSpec(memory_space=pltpu.VMEM)
    smem = pl.BlockSpec(memory_space=pltpu.SMEM)
    raw = pl.BlockSpec(memory_space=pltpu.HBM)

    features_far = pltpu.with_memory_space_constraint(features, pltpu.HBM)
    presence_far = pltpu.with_memory_space_constraint(presence, pltpu.HBM)
    send, presence = pl.pallas_call(
        prepare_kernel,
        out_shape=(
            jax.ShapeDtypeStruct((NODES, part, width), jnp.bfloat16),
            jax.ShapeDtypeStruct(presence.shape, jnp.int32),
        ),
        in_specs=[raw, raw],
        out_specs=(vmem, vmem),
        scratch_shapes=[pltpu.VMEM((part, width), jnp.bfloat16), pltpu.SemaphoreType.DMA((2,))],
        compiler_params=pltpu.CompilerParams(vmem_limit_bytes=4 << 20),
        name="prepare",
    )(features_far, presence_far)
    gathered = lax.all_to_all(
        send, EVERY, 0, 0, tiled=True, axis_index_groups=node_groups()
    )
    picked = pl.pallas_call(
        pick_kernel,
        out_shape=jax.ShapeDtypeStruct((lows, slots, part, width), jnp.bfloat16),
        in_specs=[smem, vmem],
        out_specs=vmem,
        scratch_shapes=[pltpu.VMEM((slots + 1, part, width), jnp.bfloat16)],
        compiler_params=pltpu.CompilerParams(vmem_limit_bytes=4 << 20),
        name="pick",
    )(presence, gathered)
    swap = [(0, 1), (1, 0)]
    own = lax.all_to_all(picked, "yl", 0, 0, tiled=True)
    payload = lows * slots * part + 3 * width + 16
    packed = pl.pallas_call(
        pack_kernel,
        out_shape=jax.ShapeDtypeStruct((payload, width), jnp.bfloat16),
        in_specs=[vmem] * 5,
        out_specs=vmem,
        compiler_params=pltpu.CompilerParams(vmem_limit_bytes=4 << 20),
        name="pack",
    )(own, proj_weight, out_weight, score_source, score_target)
    other = lax.ppermute(packed, "c", swap)
    cores = SIZES["c"]
    added = pl.pallas_call(
        mask_kernel,
        out_shape=jax.ShapeDtypeStruct((slots, tile, tile), jnp.float32),
        in_specs=[smem, vmem],
        out_specs=vmem,
        compiler_params=pltpu.CompilerParams(vmem_limit_bytes=4 << 20),
        cost_estimate=pl.CostEstimate(flops=slots * tile * tile, bytes_accessed=8 * slots * tile * tile, transcendentals=0),
        name="mask",
    )(presence, tile_masks)
    paired = pl.pallas_call(
        attend_kernel,
        out_shape=jax.ShapeDtypeStruct((lows, tile, out_weight.shape[1]), jnp.bfloat16),
        in_specs=[vmem] * 4,
        out_specs=vmem,
        scratch_shapes=[
            pltpu.VMEM((slots, lows, cores, part, cores * width), jnp.bfloat16),
            pltpu.VMEM((cores, 3 * width + 16, width), jnp.bfloat16),
        ],
        compiler_params=pltpu.CompilerParams(vmem_limit_bytes=16 << 20),
        name="attend",
    )(packed, other, features, added)
    pieces = lax.all_to_all(paired, "yl", 0, 0, tiled=True)
    return jnp.sum(pieces.astype(jnp.float32), axis=0).astype(jnp.bfloat16)


def solution(mesh):
    shape = tuple(SIZES[name] for name in NODE + HEAD)
    fine = Mesh(np.asarray(mesh.devices).reshape(shape), NODE + HEAD)
    return jax.shard_map(
        per_device,
        mesh=fine,
        in_specs=(
            P(NODE, None),
            P(None, HEAD),
            P(HEAD, None),
            P(HEAD, None),
            P(HEAD, None),
            P(NODE, None),
            P(NODE, None, None, None),
        ),
        out_specs=P(NODE, None),
        check_vma=False,
    )
```

```python
import functools

import jax
import jax.numpy as jnp
import numpy as np
from jax import lax
from jax.experimental import pallas as pl
from jax.experimental.pallas import tpu as pltpu
from jax.sharding import Mesh
from jax.sharding import PartitionSpec as P

NODE = ("yh", "z", "x")
HEAD = ("yl", "c")
EVERY = NODE + ("yl",)
SIZES = {"yh": 2, "z": 8, "x": 4, "yl": 4, "c": 2}
NODES = 64
EIGHTHS = 8
LOW = -1.0e38
LOG2E = 1.4426950408889634


def node_groups():
    groups = []
    for pair in range(SIZES["yl"]):
        group = []
        for yh in range(SIZES["yh"]):
            for z in range(SIZES["z"]):
                for x in range(SIZES["x"]):
                    place = (yh * SIZES["z"] + z) * SIZES["x"] + x
                    group.append(place * SIZES["yl"] + (pair ^ (2 * yh)))
        groups.append(group)
    return groups


def pair_of_device():
    return lax.axis_index("yl") ^ (2 * lax.axis_index("yh"))


def leaky_relu(values):
    return jnp.maximum(values, 0.2 * values)


def split_rows(vector):
    high = vector.astype(jnp.bfloat16).astype(jnp.float32)
    rest = vector - high
    middle = rest.astype(jnp.bfloat16).astype(jnp.float32)
    return high, middle, rest - middle


def prepare_kernel(
    features_hbm,
    presence_hbm,
    proj_hbm,
    weight_hbm,
    source_hbm,
    target_hbm,
    send_ref,
    presence_ref,
    table_ref,
    rows_ref,
    source_ref,
    target_ref,
    sems,
):
    part, width = rows_ref.shape
    start = (pair_of_device() * SIZES["c"] + lax.axis_index("c")) * part
    pairs = [
        (features_hbm.at[pl.ds(pl.multiple_of(start, part), part)], rows_ref),
        (presence_hbm, presence_ref),
        (proj_hbm, table_ref.at[:width]),
        (source_hbm, source_ref),
        (target_hbm, target_ref),
    ]
    for i in range(weight_hbm.shape[1] // width):
        pairs.append(
            (
                weight_hbm.at[:, i * width : (i + 1) * width],
                table_ref.at[(i + 1) * width : (i + 2) * width],
            )
        )
    copies = [pltpu.make_async_copy(*pair, sems.at[i]) for i, pair in enumerate(pairs)]
    for copy in copies:
        copy.start()
    copies[0].wait()
    rows = rows_ref[...]
    for i in range(send_ref.shape[0]):
        send_ref[i] = rows
    for copy in copies[1:]:
        copy.wait()
    row = lax.broadcasted_iota(jnp.int32, (16, width), 0)
    block = jnp.zeros((16, width), jnp.float32)
    for i, vector in enumerate(split_rows(source_ref[...]) + split_rows(target_ref[...])):
        block = jnp.where(row == i, vector, block)
    table_ref[3 * width :] = block.astype(jnp.bfloat16)


def pick_kernel(presence_ref, gathered_ref, out_ref, slots_ref):
    slot = jnp.int32(0)
    for tile in range(gathered_ref.shape[0]):
        slots_ref[slot] = gathered_ref[tile]
        slot = jnp.minimum(slot + presence_ref[0, tile], out_ref.shape[1])
    for i in range(out_ref.shape[1]):
        rows = slots_ref[i]
        for copy in range(out_ref.shape[0]):
            out_ref[copy, i] = rows


def pack_kernel(own_ref, table_ref, far_ref, out_ref):
    lows, slots, part, width = own_ref.shape
    rows = lows * slots * part
    size = table_ref.shape[0]
    out_ref[:rows] = own_ref[...].reshape(rows, width)
    out_ref[rows : rows + size] = table_ref[...]
    out_ref[rows + size :] = far_ref[...]


def mask_kernel(presence_ref, masks_ref, out_ref):
    _, slots, tile, _ = masks_ref.shape
    node = (lax.axis_index("yh") * SIZES["z"] + lax.axis_index("z")) * SIZES["x"] + lax.axis_index("x")
    for k in range(slots):
        out_ref[k] = jnp.where(masks_ref[0, k] == 1, 0.0, LOW)

    def count(i, rank):
        return rank + presence_ref[0, i]

    rank = lax.fori_loop(0, node, count, jnp.int32(0))

    @pl.when(presence_ref[0, node] == 1)
    def _():
        down = lax.broadcasted_iota(jnp.int32, (tile, tile), 0)
        over = lax.broadcasted_iota(jnp.int32, (tile, tile), 1)
        out_ref[rank] = jnp.where(down == over, LOW, out_ref[rank])


def attend_kernel(own_ref, other_ref, features_ref, added_ref, out_ref, values, tables):
    slots, lows, cores, part, columns = values.shape
    heads, size, width = tables.shape
    tile = added_ref.shape[1]
    share = slots * part
    rows = lows * share
    core = lax.axis_index("c")
    upper = lax.axis_index("yl") // 2
    for ref, side in ((own_ref, core), (other_ref, 1 - core)):
        tables[cores * upper + side] = ref[rows : rows + size]
        tables[cores * (1 - upper) + side] = ref[rows + size :]
    both = jnp.concatenate([tables[h, :width] for h in range(heads)], axis=1)

    def project(block):
        return jnp.dot(block, both, preferred_element_type=jnp.float32).astype(jnp.bfloat16)

    for ref, side in ((own_ref, core), (other_ref, 1 - core)):
        for low in range(lows):
            pair = low ^ (2 * lax.axis_index("yh"))
            block = project(ref[low * share : (low + 1) * share])
            values[:, pair, side] = block.reshape(slots, part, columns)

    local = project(features_ref[...]).astype(jnp.float32)
    row = lax.broadcasted_iota(jnp.int32, (8 * heads, width), 0)
    target_terms, self_source, spread = [], [], []
    for h in range(heads):
        wide = tables[h, 3 * width :].astype(jnp.float32)
        source = wide[0:1] + wide[1:2] + wide[2:3]
        target = wide[3:4] + wide[4:5] + wide[5:6]
        mine = local[:, h * width : (h + 1) * width]
        target_terms.append(LOG2E * jnp.sum(mine * target, axis=1, keepdims=True))
        self_source.append(LOG2E * jnp.sum(mine * source, axis=1, keepdims=True))
        block = jnp.zeros((8 * heads, width), jnp.float32)
        for i in range(3):
            block = jnp.where(row == 8 * h + i, wide[i : i + 1], block)
        spread.append(block)
    terms = lax.dot_general(
        jnp.concatenate(spread, axis=1).astype(jnp.bfloat16),
        values[...].reshape(slots * tile, columns),
        (((1,), (1,)), ((), ())),
        preferred_element_type=jnp.float32,
    )
    source_terms = [
        LOG2E * (terms[8 * h : 8 * h + 1] + terms[8 * h + 1 : 8 * h + 2] + terms[8 * h + 2 : 8 * h + 3])
        for h in range(heads)
    ]

    best = [jnp.full((tile, tile), LOW, jnp.float32) for h in range(heads)]
    for k in range(slots):
        added = added_ref[k]
        for h in range(heads):
            best[h] = jnp.maximum(best[h], source_terms[h][:, k * tile : (k + 1) * tile] + added)
    peaks, self_weights = [], []
    for h in range(heads):
        top = jnp.maximum(jnp.max(best[h], axis=1, keepdims=True), self_source[h])
        peaks.append(leaky_relu(target_terms[h] + top))
        self_weights.append(jnp.exp2(leaky_relu(target_terms[h] + self_source[h]) - peaks[h]))

    totals = [jnp.zeros((tile, tile), jnp.float32) for h in range(heads)]
    sums = [jnp.zeros((tile, width), jnp.float32) for h in range(heads)]
    group = 2
    for first in range(0, slots, group):
        for h in range(heads):
            edges = []
            for k in range(first, first + group):
                scores = source_terms[h][:, k * tile : (k + 1) * tile] + added_ref[k]
                edge = jnp.exp2(leaky_relu(target_terms[h] + scores) - peaks[h])
                totals[h] = totals[h] + edge
                edges.append(edge.astype(jnp.bfloat16))
            near = values[first : first + group, :, :, :, h * width : (h + 1) * width]
            sums[h] = sums[h] + jnp.dot(
                jnp.concatenate(edges, axis=1),
                near.reshape(group * tile, width),
                preferred_element_type=jnp.float32,
            )

    outs = []
    for h in range(heads):
        mine = local[:, h * width : (h + 1) * width]
        denominator = jnp.sum(totals[h], axis=1, keepdims=True) + self_weights[h]
        summed = sums[h] + self_weights[h].astype(jnp.bfloat16).astype(jnp.float32) * mine
        attended = summed / denominator
        below = jnp.minimum(attended, 0.0)
        bent = jnp.tanh(0.5 * below)
        outs.append(jnp.where(attended > 0, attended, 2.0 * bent / (1.0 - bent)).astype(jnp.bfloat16))
    joined = jnp.concatenate(outs, axis=1)
    columns = []
    for i in (1, 2):
        table = jnp.concatenate(
            [tables[h, i * width : (i + 1) * width] for h in range(heads)], axis=0
        )
        columns.append(jnp.dot(joined, table, preferred_element_type=jnp.float32))
    mixed = jnp.concatenate(columns, axis=1).astype(jnp.bfloat16)
    out_ref[...] = mixed


def per_device(features, proj_weight, score_source, score_target, out_weight, presence, tile_masks):
    tile, width = features.shape
    slots = tile_masks.shape[1]
    part = tile // EIGHTHS
    lows = SIZES["yl"]
    vmem = pl.BlockSpec(memory_space=pltpu.VMEM)
    smem = pl.BlockSpec(memory_space=pltpu.SMEM)
    raw = pl.BlockSpec(memory_space=pltpu.HBM)

    far = [
        pltpu.with_memory_space_constraint(value, pltpu.HBM)
        for value in (features, presence, proj_weight, out_weight, score_source, score_target)
    ]
    size = width + out_weight.shape[1] + 16
    send, presence, table = pl.pallas_call(
        prepare_kernel,
        out_shape=(
            jax.ShapeDtypeStruct((NODES, part, width), jnp.bfloat16),
            jax.ShapeDtypeStruct(presence.shape, jnp.int32),
            jax.ShapeDtypeStruct((size, width), jnp.bfloat16),
        ),
        in_specs=[raw] * 6,
        out_specs=(vmem,) * 3,
        scratch_shapes=[
            pltpu.VMEM((part, width), jnp.bfloat16),
            pltpu.VMEM(score_source.shape, jnp.float32),
            pltpu.VMEM(score_target.shape, jnp.float32),
            pltpu.SemaphoreType.DMA((7,)),
        ],
        compiler_params=pltpu.CompilerParams(vmem_limit_bytes=4 << 20),
        name="prepare",
    )(*far)
    far_table = lax.ppermute(table, "yl", [(i, i ^ 2) for i in range(lows)])
    gathered = lax.all_to_all(
        send, EVERY, 0, 0, tiled=True, axis_index_groups=node_groups()
    )
    gathered, far_table = lax.optimization_barrier((gathered, far_table))
    picked = pl.pallas_call(
        pick_kernel,
        out_shape=jax.ShapeDtypeStruct((lows, slots, part, width), jnp.bfloat16),
        in_specs=[smem, vmem],
        out_specs=vmem,
        scratch_shapes=[pltpu.VMEM((slots + 1, part, width), jnp.bfloat16)],
        compiler_params=pltpu.CompilerParams(vmem_limit_bytes=4 << 20),
        name="pick",
    )(presence, gathered)
    swap = [(0, 1), (1, 0)]
    own = lax.all_to_all(picked, "yl", 0, 0, tiled=True)
    packed = pl.pallas_call(
        pack_kernel,
        out_shape=jax.ShapeDtypeStruct((lows * slots * part + 2 * size, width), jnp.bfloat16),
        in_specs=[vmem] * 3,
        out_specs=vmem,
        compiler_params=pltpu.CompilerParams(vmem_limit_bytes=4 << 20),
        name="pack",
    )(own, table, far_table)
    other = lax.ppermute(packed, "c", swap)
    cores = SIZES["c"]
    added = pl.pallas_call(
        mask_kernel,
        out_shape=jax.ShapeDtypeStruct((slots, tile, tile), jnp.float32),
        in_specs=[smem, vmem],
        out_specs=vmem,
        compiler_params=pltpu.CompilerParams(vmem_limit_bytes=4 << 20),
        cost_estimate=pl.CostEstimate(flops=slots * tile * tile, bytes_accessed=8 * slots * tile * tile, transcendentals=0),
        name="mask",
    )(presence, tile_masks)
    partial = pl.pallas_call(
        attend_kernel,
        out_shape=jax.ShapeDtypeStruct((tile, out_weight.shape[1]), jnp.bfloat16),
        in_specs=[vmem] * 4,
        out_specs=vmem,
        scratch_shapes=[
            pltpu.VMEM((slots, lows, cores, part, 2 * cores * width), jnp.bfloat16),
            pltpu.VMEM((2 * cores, size, width), jnp.bfloat16),
        ],
        compiler_params=pltpu.CompilerParams(vmem_limit_bytes=16 << 20),
        name="attend",
    )(packed, other, features, added)
    beside = lax.ppermute(partial, "yl", [(i, i ^ 1) for i in range(lows)])
    return (partial.astype(jnp.float32) + beside.astype(jnp.float32)).astype(jnp.bfloat16)


def solution(mesh):
    shape = tuple(SIZES[name] for name in NODE + HEAD)
    fine = Mesh(np.asarray(mesh.devices).reshape(shape), NODE + HEAD)
    return jax.shard_map(
        per_device,
        mesh=fine,
        in_specs=(
            P(NODE, None),
            P(None, HEAD),
            P(HEAD, None),
            P(HEAD, None),
            P(HEAD, None),
            P(NODE, None),
            P(NODE, None, None, None),
        ),
        out_specs=P(NODE, None),
        check_vma=False,
    )
```

```python
import functools

import jax
import jax.numpy as jnp
import numpy as np
from jax import lax
from jax.experimental import pallas as pl
from jax.experimental.pallas import tpu as pltpu
from jax.sharding import Mesh
from jax.sharding import PartitionSpec as P

NODE = ("yh", "z", "x")
HEAD = ("yl", "c")
EVERY = NODE + ("yl",)
SIZES = {"yh": 2, "z": 8, "x": 4, "yl": 4, "c": 2}
NODES = 64
EIGHTHS = 8
LOW = -1.0e38
LOG2E = 1.4426950408889634


def node_groups():
    groups = []
    for pair in range(SIZES["yl"]):
        group = []
        for yh in range(SIZES["yh"]):
            for z in range(SIZES["z"]):
                for x in range(SIZES["x"]):
                    place = (yh * SIZES["z"] + z) * SIZES["x"] + x
                    group.append(place * SIZES["yl"] + (pair ^ (2 * yh)))
        groups.append(group)
    return groups


def square_groups():
    groups = []
    for plane in range(SIZES["yh"] * SIZES["z"]):
        for x in range(0, SIZES["x"], 2):
            for yl in range(0, SIZES["yl"], 2):
                groups.append(
                    [
                        (plane * SIZES["x"] + x + i) * SIZES["yl"] + yl + j
                        for i in range(2)
                        for j in range(2)
                    ]
                )
    return groups


def leaky_relu(values):
    return jnp.maximum(values, 0.2 * values)


def split_rows(vector):
    high = vector.astype(jnp.bfloat16).astype(jnp.float32)
    rest = vector - high
    middle = rest.astype(jnp.bfloat16).astype(jnp.float32)
    return high, middle, rest - middle


def send_kernel(features_hbm, send_ref, rows_ref, sems):
    sides, part, width = rows_ref.shape
    first = (lax.rem(lax.axis_index("yl"), 2) * SIZES["c"] + lax.axis_index("c")) * part
    copies = []
    for side in range(sides):
        start = pl.multiple_of(first + side * (features_hbm.shape[0] // sides), part)
        copies.append(
            pltpu.make_async_copy(
                features_hbm.at[pl.ds(start, part)], rows_ref.at[side], sems.at[side]
            )
        )
        copies[-1].start()
    for copy in copies:
        copy.wait()
    for i in range(send_ref.shape[0]):
        send_ref[i] = rows_ref[i % sides]


def table_kernel(
    proj_hbm, weight_hbm, source_hbm, target_hbm, table_ref, source_ref, target_ref, sems
):
    width = table_ref.shape[1]
    pairs = [(proj_hbm, table_ref.at[:width]), (source_hbm, source_ref), (target_hbm, target_ref)]
    for i in range(weight_hbm.shape[1] // width):
        pairs.append(
            (
                weight_hbm.at[:, i * width : (i + 1) * width],
                table_ref.at[(i + 1) * width : (i + 2) * width],
            )
        )
    copies = [pltpu.make_async_copy(*pair, sems.at[i]) for i, pair in enumerate(pairs)]
    for copy in copies:
        copy.start()
    for copy in copies:
        copy.wait()
    row = lax.broadcasted_iota(jnp.int32, (16, width), 0)
    block = jnp.zeros((16, width), jnp.float32)
    for i, vector in enumerate(split_rows(source_ref[...]) + split_rows(target_ref[...])):
        block = jnp.where(row == i, vector, block)
    table_ref[3 * width :] = block.astype(jnp.bfloat16)


def pick_kernel(presence_ref, near_ref, gathered_ref, out_ref, slots_ref):
    members, slots = out_ref.shape[:2]
    ends = [jnp.int32(0), jnp.int32(0)]
    for tile in range(gathered_ref.shape[0]):
        rows = gathered_ref[tile]
        for i, ref in enumerate((presence_ref, near_ref)):
            slots_ref[i, ends[i]] = rows
            ends[i] = jnp.minimum(ends[i] + ref[0, tile], slots)
    odd = lax.rem(lax.axis_index("x"), 2)
    for member in range(members):
        row = odd ^ (member // 2)
        for k in range(slots):
            out_ref[member, k] = slots_ref[row, k]


def pack_kernel(own_ref, table_ref, far_ref, out_ref):
    lows, slots, part, width = own_ref.shape
    rows = lows * slots * part
    size = table_ref.shape[0]
    out_ref[:rows] = own_ref[...].reshape(rows, width)
    out_ref[rows : rows + size] = table_ref[...]
    out_ref[rows + size :] = far_ref[...]


def mask_kernel(presence_ref, masks_ref, out_ref):
    _, slots, tile, _ = masks_ref.shape
    node = (lax.axis_index("yh") * SIZES["z"] + lax.axis_index("z")) * SIZES["x"] + lax.axis_index("x")
    for k in range(slots):
        out_ref[k] = jnp.where(masks_ref[0, k] == 1, 0.0, LOW)

    def count(i, rank):
        return rank + presence_ref[0, i]

    rank = lax.fori_loop(0, node, count, jnp.int32(0))

    @pl.when(presence_ref[0, node] == 1)
    def _():
        down = lax.broadcasted_iota(jnp.int32, (tile, tile), 0)
        over = lax.broadcasted_iota(jnp.int32, (tile, tile), 1)
        out_ref[rank] = jnp.where(down == over, LOW, out_ref[rank])


def attend_kernel(own_ref, other_ref, features_ref, added_ref, out_ref, values, tables):
    slots, lows, cores, part, columns = values.shape
    heads, size, width = tables.shape
    tile = added_ref.shape[1]
    share = slots * part
    rows = lows * share
    core = lax.axis_index("c")
    upper = lax.axis_index("yl") // 2
    for ref, side in ((own_ref, core), (other_ref, 1 - core)):
        tables[cores * upper + side] = ref[rows : rows + size]
        tables[cores * (1 - upper) + side] = ref[rows + size :]
    both = jnp.concatenate([tables[h, :width] for h in range(heads)], axis=1)

    def project(block):
        return jnp.dot(block, both, preferred_element_type=jnp.float32).astype(jnp.bfloat16)

    for ref, side in ((own_ref, core), (other_ref, 1 - core)):
        for low in range(lows):
            block = project(ref[low * share : (low + 1) * share])
            values[:, low, side] = block.reshape(slots, part, columns)

    local = project(features_ref[...]).astype(jnp.float32)
    row = lax.broadcasted_iota(jnp.int32, (8 * heads, width), 0)
    target_terms, self_source, spread = [], [], []
    for h in range(heads):
        wide = tables[h, 3 * width :].astype(jnp.float32)
        source = wide[0:1] + wide[1:2] + wide[2:3]
        target = wide[3:4] + wide[4:5] + wide[5:6]
        mine = local[:, h * width : (h + 1) * width]
        target_terms.append(LOG2E * jnp.sum(mine * target, axis=1, keepdims=True))
        self_source.append(LOG2E * jnp.sum(mine * source, axis=1, keepdims=True))
        block = jnp.zeros((8 * heads, width), jnp.float32)
        for i in range(3):
            block = jnp.where(row == 8 * h + i, wide[i : i + 1], block)
        spread.append(block)
    terms = lax.dot_general(
        jnp.concatenate(spread, axis=1).astype(jnp.bfloat16),
        values[...].reshape(slots * tile, columns),
        (((1,), (1,)), ((), ())),
        preferred_element_type=jnp.float32,
    )
    source_terms = [
        LOG2E * (terms[8 * h : 8 * h + 1] + terms[8 * h + 1 : 8 * h + 2] + terms[8 * h + 2 : 8 * h + 3])
        for h in range(heads)
    ]

    best = [jnp.full((tile, tile), LOW, jnp.float32) for h in range(heads)]
    for k in range(slots):
        added = added_ref[k]
        for h in range(heads):
            best[h] = jnp.maximum(best[h], source_terms[h][:, k * tile : (k + 1) * tile] + added)
    peaks, self_weights = [], []
    for h in range(heads):
        top = jnp.maximum(jnp.max(best[h], axis=1, keepdims=True), self_source[h])
        peaks.append(leaky_relu(target_terms[h] + top))
        self_weights.append(jnp.exp2(leaky_relu(target_terms[h] + self_source[h]) - peaks[h]))

    totals = [jnp.zeros((tile, tile), jnp.float32) for h in range(heads)]
    sums = [jnp.zeros((tile, width), jnp.float32) for h in range(heads)]
    group = 2
    for first in range(0, slots, group):
        for h in range(heads):
            edges = []
            for k in range(first, first + group):
                scores = source_terms[h][:, k * tile : (k + 1) * tile] + added_ref[k]
                edge = jnp.exp2(leaky_relu(target_terms[h] + scores) - peaks[h])
                totals[h] = totals[h] + edge
                edges.append(edge.astype(jnp.bfloat16))
            near = values[first : first + group, :, :, :, h * width : (h + 1) * width]
            sums[h] = sums[h] + jnp.dot(
                jnp.concatenate(edges, axis=1),
                near.reshape(group * tile, width),
                preferred_element_type=jnp.float32,
            )

    outs = []
    for h in range(heads):
        mine = local[:, h * width : (h + 1) * width]
        denominator = jnp.sum(totals[h], axis=1, keepdims=True) + self_weights[h]
        summed = sums[h] + self_weights[h].astype(jnp.bfloat16).astype(jnp.float32) * mine
        attended = summed / denominator
        below = jnp.minimum(attended, 0.0)
        bent = jnp.tanh(0.5 * below)
        outs.append(jnp.where(attended > 0, attended, 2.0 * bent / (1.0 - bent)).astype(jnp.bfloat16))
    joined = jnp.concatenate(outs, axis=1)
    columns = []
    for i in (1, 2):
        table = jnp.concatenate(
            [tables[h, i * width : (i + 1) * width] for h in range(heads)], axis=0
        )
        columns.append(jnp.dot(joined, table, preferred_element_type=jnp.float32))
    mixed = jnp.concatenate(columns, axis=1).astype(jnp.bfloat16)
    out_ref[...] = mixed


def per_device(features, proj_weight, score_source, score_target, out_weight, presence, tile_masks):
    tile, width = features.shape
    slots = tile_masks.shape[1]
    part = tile // EIGHTHS
    lows = SIZES["yl"]
    vmem = pl.BlockSpec(memory_space=pltpu.VMEM)
    smem = pl.BlockSpec(memory_space=pltpu.SMEM)
    raw = pl.BlockSpec(memory_space=pltpu.HBM)

    far = [
        pltpu.with_memory_space_constraint(value, pltpu.HBM)
        for value in (features, proj_weight, out_weight, score_source, score_target)
    ]
    size = width + out_weight.shape[1] + 16
    send = pl.pallas_call(
        send_kernel,
        out_shape=jax.ShapeDtypeStruct((NODES, part, width), jnp.bfloat16),
        in_specs=[raw],
        out_specs=vmem,
        scratch_shapes=[pltpu.VMEM((2, part, width), jnp.bfloat16), pltpu.SemaphoreType.DMA((2,))],
        compiler_params=pltpu.CompilerParams(vmem_limit_bytes=4 << 20),
        name="send",
    )(far[0])
    table = pl.pallas_call(
        table_kernel,
        out_shape=jax.ShapeDtypeStruct((size, width), jnp.bfloat16),
        in_specs=[raw] * 4,
        out_specs=vmem,
        scratch_shapes=[
            pltpu.VMEM(score_source.shape, jnp.float32),
            pltpu.VMEM(score_target.shape, jnp.float32),
            pltpu.SemaphoreType.DMA((5,)),
        ],
        compiler_params=pltpu.CompilerParams(vmem_limit_bytes=4 << 20),
        cost_estimate=pl.CostEstimate(flops=0, bytes_accessed=4 * size * width, transcendentals=0),
        name="table",
    )(*far[1:])
    far_table = lax.ppermute(table, "yl", [(i, i ^ 2) for i in range(lows)])
    near = lax.ppermute(presence, "x", [(i, i ^ 1) for i in range(SIZES["x"])])
    gathered = lax.all_to_all(
        send, EVERY, 0, 0, tiled=True, axis_index_groups=node_groups()
    )
    gathered, far_table, near = lax.optimization_barrier((gathered, far_table, near))
    picked = pl.pallas_call(
        pick_kernel,
        out_shape=jax.ShapeDtypeStruct((lows, slots, part, width), jnp.bfloat16),
        in_specs=[smem, smem, vmem],
        out_specs=vmem,
        scratch_shapes=[pltpu.VMEM((2, slots + 1, part, width), jnp.bfloat16)],
        compiler_params=pltpu.CompilerParams(vmem_limit_bytes=4 << 20),
        name="pick",
    )(presence, near, gathered)
    swap = [(0, 1), (1, 0)]
    own = lax.all_to_all(
        picked, EVERY, 0, 0, tiled=True, axis_index_groups=square_groups()
    )
    packed = pl.pallas_call(
        pack_kernel,
        out_shape=jax.ShapeDtypeStruct((lows * slots * part + 2 * size, width), jnp.bfloat16),
        in_specs=[vmem] * 3,
        out_specs=vmem,
        compiler_params=pltpu.CompilerParams(vmem_limit_bytes=4 << 20),
        name="pack",
    )(own, table, far_table)
    other = lax.ppermute(packed, "c", swap)
    cores = SIZES["c"]
    added = pl.pallas_call(
        mask_kernel,
        out_shape=jax.ShapeDtypeStruct((slots, tile, tile), jnp.float32),
        in_specs=[smem, vmem],
        out_specs=vmem,
        compiler_params=pltpu.CompilerParams(vmem_limit_bytes=4 << 20),
        cost_estimate=pl.CostEstimate(flops=slots * tile * tile, bytes_accessed=8 * slots * tile * tile, transcendentals=0),
        name="mask",
    )(presence, tile_masks)
    partial = pl.pallas_call(
        attend_kernel,
        out_shape=jax.ShapeDtypeStruct((tile, out_weight.shape[1]), jnp.bfloat16),
        in_specs=[vmem] * 4,
        out_specs=vmem,
        scratch_shapes=[
            pltpu.VMEM((slots, lows, cores, part, 2 * cores * width), jnp.bfloat16),
            pltpu.VMEM((2 * cores, size, width), jnp.bfloat16),
        ],
        compiler_params=pltpu.CompilerParams(vmem_limit_bytes=16 << 20),
        name="attend",
    )(packed, other, features, added)
    beside = lax.ppermute(partial, "yl", [(i, i ^ 1) for i in range(lows)])
    return (partial.astype(jnp.float32) + beside.astype(jnp.float32)).astype(jnp.bfloat16)


def solution(mesh):
    shape = tuple(SIZES[name] for name in NODE + HEAD)
    fine = Mesh(np.asarray(mesh.devices).reshape(shape), NODE + HEAD)
    return jax.shard_map(
        per_device,
        mesh=fine,
        in_specs=(
            P(NODE, None),
            P(None, HEAD),
            P(HEAD, None),
            P(HEAD, None),
            P(HEAD, None),
            P(NODE, None),
            P(NODE, None, None, None),
        ),
        out_specs=P(NODE, None),
        check_vma=False,
    )
```

```python
import functools

import jax
import jax.numpy as jnp
import numpy as np
from jax import lax
from jax.experimental import pallas as pl
from jax.experimental.pallas import tpu as pltpu
from jax.sharding import Mesh
from jax.sharding import PartitionSpec as P

NODE = ("yh", "z", "x")
HEAD = ("yl", "c")
EVERY = NODE + ("yl",)
SIZES = {"yh": 2, "z": 8, "x": 4, "yl": 4, "c": 2}
NODES = 64
EIGHTHS = 8
LOW = -1.0e38
LOG2E = 1.4426950408889634


def node_groups():
    groups = []
    for pair in range(SIZES["yl"]):
        group = []
        for yh in range(SIZES["yh"]):
            for z in range(SIZES["z"]):
                for x in range(SIZES["x"]):
                    place = (yh * SIZES["z"] + z) * SIZES["x"] + x
                    group.append(place * SIZES["yl"] + (pair ^ (2 * yh)))
        groups.append(group)
    return groups


def square_groups():
    groups = []
    for plane in range(SIZES["yh"] * SIZES["z"]):
        for x in range(0, SIZES["x"], 2):
            for yl in range(0, SIZES["yl"], 2):
                groups.append(
                    [
                        (plane * SIZES["x"] + x + i) * SIZES["yl"] + yl + j
                        for i in range(2)
                        for j in range(2)
                    ]
                )
    return groups


def leaky_relu(values):
    return jnp.maximum(values, 0.2 * values)


def split_rows(vector):
    high = vector.astype(jnp.bfloat16).astype(jnp.float32)
    rest = vector - high
    middle = rest.astype(jnp.bfloat16).astype(jnp.float32)
    return high, middle, rest - middle


def send_kernel(features_hbm, send_ref, rows_ref, sems):
    sides, part, width = rows_ref.shape
    first = (lax.rem(lax.axis_index("yl"), 2) * SIZES["c"] + lax.axis_index("c")) * part
    copies = []
    for side in range(sides):
        start = pl.multiple_of(first + side * (features_hbm.shape[0] // sides), part)
        copies.append(
            pltpu.make_async_copy(
                features_hbm.at[pl.ds(start, part)], rows_ref.at[side], sems.at[side]
            )
        )
        copies[-1].start()
    for copy in copies:
        copy.wait()
    for i in range(send_ref.shape[0]):
        send_ref[i] = rows_ref[i % sides]


def table_kernel(
    proj_hbm, weight_hbm, source_hbm, target_hbm, presence_hbm, table_ref, source_ref, target_ref, row_ref, sems
):
    width = table_ref.shape[1]
    pairs = [(proj_hbm, table_ref.at[:width]), (source_hbm, source_ref), (target_hbm, target_ref)]
    pairs.append((presence_hbm, row_ref))
    for i in range(weight_hbm.shape[1] // width):
        pairs.append(
            (
                weight_hbm.at[:, i * width : (i + 1) * width],
                table_ref.at[(i + 1) * width : (i + 2) * width],
            )
        )
    copies = [pltpu.make_async_copy(*pair, sems.at[i]) for i, pair in enumerate(pairs)]
    for copy in copies:
        copy.start()
    for copy in copies:
        copy.wait()
    row = lax.broadcasted_iota(jnp.int32, (16, width), 0)
    block = jnp.zeros((16, width), jnp.float32)
    for i, vector in enumerate(split_rows(source_ref[...]) + split_rows(target_ref[...])):
        block = jnp.where(row == i, vector, block)
    table_ref[3 * width : 3 * width + 16] = block.astype(jnp.bfloat16)
    table_ref[3 * width + 16 :] = jnp.zeros((16, width), jnp.bfloat16)
    table_ref[3 * width + 16 :, : row_ref.shape[1]] = jnp.broadcast_to(
        row_ref[...].astype(jnp.float32), (16, row_ref.shape[1])
    ).astype(jnp.bfloat16)


def pick_kernel(presence_ref, near_ref, gathered_ref, out_ref, slots_ref):
    members, slots = out_ref.shape[:2]
    ends = [jnp.int32(0), jnp.int32(0)]
    for tile in range(gathered_ref.shape[0]):
        rows = gathered_ref[tile]
        for i, ref in enumerate((presence_ref, near_ref)):
            slots_ref[i, ends[i]] = rows
            ends[i] = jnp.minimum(ends[i] + ref[0, tile], slots)
    odd = lax.rem(lax.axis_index("x"), 2)
    for member in range(members):
        row = odd ^ (member // 2)
        for k in range(slots):
            out_ref[member, k] = slots_ref[row, k]


def pack_kernel(own_ref, *refs):
    tables, out_ref = refs[:-1], refs[-1]
    lows, slots, part, width = own_ref.shape
    rows = lows * slots * part
    size = tables[0].shape[0]
    out_ref[:rows] = own_ref[...].reshape(rows, width)
    for i, ref in enumerate(tables):
        out_ref[rows + i * size : rows + (i + 1) * size] = ref[...]


def mask_kernel(presence_ref, masks_ref, out_ref):
    _, slots, tile, _ = masks_ref.shape
    node = (lax.axis_index("yh") * SIZES["z"] + lax.axis_index("z")) * SIZES["x"] + lax.axis_index("x")
    for k in range(slots):
        out_ref[k] = jnp.where(masks_ref[0, k] == 1, 0.0, LOW)

    def count(i, rank):
        return rank + presence_ref[0, i]

    rank = lax.fori_loop(0, node, count, jnp.int32(0))

    @pl.when(presence_ref[0, node] == 1)
    def _():
        down = lax.broadcasted_iota(jnp.int32, (tile, tile), 0)
        over = lax.broadcasted_iota(jnp.int32, (tile, tile), 1)
        out_ref[rank] = jnp.where(down == over, LOW, out_ref[rank])


def attend_kernel(own_ref, other_ref, features_ref, added_ref, out_ref, values, tables):
    slots, lows, cores, part, columns = values.shape
    heads, size, width = tables.shape
    tile = added_ref.shape[1]
    share = slots * part
    rows = lows * share
    core = lax.axis_index("c")
    for ref, side in ((own_ref, core), (other_ref, 1 - core)):
        for flip in range(lows):
            start = rows + flip * size
            tables[cores * (lax.axis_index("yl") ^ flip) + side] = ref[start : start + size]
    both = jnp.concatenate([tables[h, :width] for h in range(heads)], axis=1)

    def project(block):
        return jnp.dot(block, both, preferred_element_type=jnp.float32).astype(jnp.bfloat16)

    for ref, side in ((own_ref, core), (other_ref, 1 - core)):
        for low in range(lows):
            block = project(ref[low * share : (low + 1) * share])
            values[:, low, side] = block.reshape(slots, part, columns)

    local = project(features_ref[...]).astype(jnp.float32)
    row = lax.broadcasted_iota(jnp.int32, (8 * heads, width), 0)
    target_terms, self_source, spread = [], [], []
    for h in range(heads):
        wide = tables[h, 3 * width : 3 * width + 16].astype(jnp.float32)
        source = wide[0:1] + wide[1:2] + wide[2:3]
        target = wide[3:4] + wide[4:5] + wide[5:6]
        mine = local[:, h * width : (h + 1) * width]
        target_terms.append(LOG2E * jnp.sum(mine * target, axis=1, keepdims=True))
        self_source.append(LOG2E * jnp.sum(mine * source, axis=1, keepdims=True))
        block = jnp.zeros((8 * heads, width), jnp.float32)
        for i in range(3):
            block = jnp.where(row == 8 * h + i, wide[i : i + 1], block)
        spread.append(block)
    terms = lax.dot_general(
        jnp.concatenate(spread, axis=1).astype(jnp.bfloat16),
        values[...].reshape(slots * tile, columns),
        (((1,), (1,)), ((), ())),
        preferred_element_type=jnp.float32,
    )
    source_terms = [
        LOG2E * (terms[8 * h : 8 * h + 1] + terms[8 * h + 1 : 8 * h + 2] + terms[8 * h + 2 : 8 * h + 3])
        for h in range(heads)
    ]

    best = [jnp.full((tile, tile), LOW, jnp.float32) for h in range(heads)]
    for k in range(slots):
        added = added_ref[k]
        for h in range(heads):
            best[h] = jnp.maximum(best[h], source_terms[h][:, k * tile : (k + 1) * tile] + added)
    peaks, self_weights = [], []
    for h in range(heads):
        top = jnp.maximum(jnp.max(best[h], axis=1, keepdims=True), self_source[h])
        peaks.append(leaky_relu(target_terms[h] + top))
        self_weights.append(jnp.exp2(leaky_relu(target_terms[h] + self_source[h]) - peaks[h]))

    totals = [jnp.zeros((tile, tile), jnp.float32) for h in range(heads)]
    sums = [jnp.zeros((tile, width), jnp.float32) for h in range(heads)]
    group = 2
    for first in range(0, slots, group):
        for h in range(heads):
            edges = []
            for k in range(first, first + group):
                scores = source_terms[h][:, k * tile : (k + 1) * tile] + added_ref[k]
                edge = jnp.exp2(leaky_relu(target_terms[h] + scores) - peaks[h])
                totals[h] = totals[h] + edge
                edges.append(edge.astype(jnp.bfloat16))
            near = values[first : first + group, :, :, :, h * width : (h + 1) * width]
            sums[h] = sums[h] + jnp.dot(
                jnp.concatenate(edges, axis=1),
                near.reshape(group * tile, width),
                preferred_element_type=jnp.float32,
            )

    outs = []
    for h in range(heads):
        mine = local[:, h * width : (h + 1) * width]
        denominator = jnp.sum(totals[h], axis=1, keepdims=True) + self_weights[h]
        summed = sums[h] + self_weights[h].astype(jnp.bfloat16).astype(jnp.float32) * mine
        attended = summed / denominator
        below = jnp.minimum(attended, 0.0)
        bent = jnp.tanh(0.5 * below)
        outs.append(jnp.where(attended > 0, attended, 2.0 * bent / (1.0 - bent)).astype(jnp.bfloat16))
    joined = jnp.concatenate(outs, axis=1)
    columns = []
    for i in (1, 2):
        table = jnp.concatenate(
            [tables[h, i * width : (i + 1) * width] for h in range(heads)], axis=0
        )
        columns.append(jnp.dot(joined, table, preferred_element_type=jnp.float32))
    mixed = jnp.concatenate(columns, axis=1).astype(jnp.bfloat16)
    out_ref[...] = mixed


def per_device(features, proj_weight, score_source, score_target, out_weight, presence, tile_masks):
    tile, width = features.shape
    slots = tile_masks.shape[1]
    part = tile // EIGHTHS
    lows = SIZES["yl"]
    vmem = pl.BlockSpec(memory_space=pltpu.VMEM)
    smem = pl.BlockSpec(memory_space=pltpu.SMEM)
    raw = pl.BlockSpec(memory_space=pltpu.HBM)

    far = [
        pltpu.with_memory_space_constraint(value, pltpu.HBM)
        for value in (features, proj_weight, out_weight, score_source, score_target, presence)
    ]
    size = width + out_weight.shape[1] + 32
    send = pl.pallas_call(
        send_kernel,
        out_shape=jax.ShapeDtypeStruct((NODES, part, width), jnp.bfloat16),
        in_specs=[raw],
        out_specs=vmem,
        scratch_shapes=[pltpu.VMEM((2, part, width), jnp.bfloat16), pltpu.SemaphoreType.DMA((2,))],
        compiler_params=pltpu.CompilerParams(vmem_limit_bytes=4 << 20),
        name="send",
    )(far[0])
    table = pl.pallas_call(
        table_kernel,
        out_shape=jax.ShapeDtypeStruct((size, width), jnp.bfloat16),
        in_specs=[raw] * 5,
        out_specs=vmem,
        scratch_shapes=[
            pltpu.VMEM(score_source.shape, jnp.float32),
            pltpu.VMEM(score_target.shape, jnp.float32),
            pltpu.VMEM(presence.shape, jnp.int32),
            pltpu.SemaphoreType.DMA((6,)),
        ],
        compiler_params=pltpu.CompilerParams(vmem_limit_bytes=4 << 20),
        cost_estimate=pl.CostEstimate(flops=0, bytes_accessed=4 * size * width, transcendentals=0),
        name="table",
    )(*far[1:])
    diagonal = [
        (x * lows + yl, (x ^ 1) * lows + (yl ^ 2)) for x in range(SIZES["x"]) for yl in range(lows)
    ]
    tables = {0: table, 2: lax.ppermute(table, ("x", "yl"), diagonal)}
    for flip in (1, 3):
        tables[flip] = lax.ppermute(table, "yl", [(i, i ^ flip) for i in range(lows)])
    near = tables[2][size - 16 : size - 15, : presence.shape[1]].astype(jnp.int32)
    gathered = lax.all_to_all(
        send, EVERY, 0, 0, tiled=True, axis_index_groups=node_groups()
    )
    gathered, near = lax.optimization_barrier((gathered, near))
    picked = pl.pallas_call(
        pick_kernel,
        out_shape=jax.ShapeDtypeStruct((lows, slots, part, width), jnp.bfloat16),
        in_specs=[smem, smem, vmem],
        out_specs=vmem,
        scratch_shapes=[pltpu.VMEM((2, slots + 1, part, width), jnp.bfloat16)],
        compiler_params=pltpu.CompilerParams(vmem_limit_bytes=4 << 20),
        name="pick",
    )(presence, near, gathered)
    swap = [(0, 1), (1, 0)]
    picked, tables = lax.optimization_barrier((picked, tables))
    own = lax.all_to_all(
        picked, EVERY, 0, 0, tiled=True, axis_index_groups=square_groups()
    )
    packed = pl.pallas_call(
        pack_kernel,
        out_shape=jax.ShapeDtypeStruct((lows * slots * part + 4 * size, width), jnp.bfloat16),
        in_specs=[vmem] * 5,
        out_specs=vmem,
        compiler_params=pltpu.CompilerParams(vmem_limit_bytes=4 << 20),
        name="pack",
    )(own, *[tables[flip] for flip in range(4)])
    other = lax.ppermute(packed, "c", swap)
    cores = SIZES["c"]
    added = pl.pallas_call(
        mask_kernel,
        out_shape=jax.ShapeDtypeStruct((slots, tile, tile), jnp.float32),
        in_specs=[smem, vmem],
        out_specs=vmem,
        compiler_params=pltpu.CompilerParams(vmem_limit_bytes=4 << 20),
        cost_estimate=pl.CostEstimate(flops=slots * tile * tile, bytes_accessed=8 * slots * tile * tile, transcendentals=0),
        name="mask",
    )(presence, tile_masks)
    return pl.pallas_call(
        attend_kernel,
        out_shape=jax.ShapeDtypeStruct((tile, out_weight.shape[1]), jnp.bfloat16),
        in_specs=[vmem] * 4,
        out_specs=vmem,
        scratch_shapes=[
            pltpu.VMEM((slots, lows, cores, part, lows * cores * width), jnp.bfloat16),
            pltpu.VMEM((lows * cores, size, width), jnp.bfloat16),
        ],
        compiler_params=pltpu.CompilerParams(vmem_limit_bytes=16 << 20),
        name="attend",
    )(packed, other, features, added)


def solution(mesh):
    shape = tuple(SIZES[name] for name in NODE + HEAD)
    fine = Mesh(np.asarray(mesh.devices).reshape(shape), NODE + HEAD)
    return jax.shard_map(
        per_device,
        mesh=fine,
        in_specs=(
            P(NODE, None),
            P(None, HEAD),
            P(HEAD, None),
            P(HEAD, None),
            P(HEAD, None),
            P(NODE, None),
            P(NODE, None, None, None),
        ),
        out_specs=P(NODE, None),
        check_vma=False,
    )
```

```python
import functools

import jax
import jax.numpy as jnp
import numpy as np
from jax import lax
from jax.experimental import pallas as pl
from jax.experimental.pallas import tpu as pltpu
from jax.sharding import Mesh
from jax.sharding import PartitionSpec as P

NODE = ("yh", "z", "x")
HEAD = ("yl", "c")
EVERY = NODE + ("yl",)
SIZES = {"yh": 2, "z": 8, "x": 4, "yl": 4, "c": 2}
NODES = 64
EIGHTHS = 8
LOW = -1.0e38
LOG2E = 1.4426950408889634


def node_groups():
    groups = []
    for pair in range(SIZES["yl"]):
        group = []
        for yh in range(SIZES["yh"]):
            for z in range(SIZES["z"]):
                for x in range(SIZES["x"]):
                    place = (yh * SIZES["z"] + z) * SIZES["x"] + x
                    group.append(place * SIZES["yl"] + (pair ^ (2 * yh)))
        groups.append(group)
    return groups


def square_groups():
    groups = []
    for plane in range(SIZES["yh"] * SIZES["z"]):
        for x in range(0, SIZES["x"], 2):
            for yl in range(0, SIZES["yl"], 2):
                groups.append(
                    [
                        (plane * SIZES["x"] + x + i) * SIZES["yl"] + yl + j
                        for i in range(2)
                        for j in range(2)
                    ]
                )
    return groups


def leaky_relu(values):
    return jnp.maximum(values, 0.2 * values)


def split_rows(vector):
    high = vector.astype(jnp.bfloat16).astype(jnp.float32)
    rest = vector - high
    middle = rest.astype(jnp.bfloat16).astype(jnp.float32)
    return high, middle, rest - middle


def send_kernel(features_hbm, send_ref, rows_ref, sems):
    sides, part, width = rows_ref.shape
    first = (lax.rem(lax.axis_index("yl"), 2) * SIZES["c"] + lax.axis_index("c")) * part
    copies = []
    for side in range(sides):
        start = pl.multiple_of(first + side * (features_hbm.shape[0] // sides), part)
        copies.append(
            pltpu.make_async_copy(
                features_hbm.at[pl.ds(start, part)], rows_ref.at[side], sems.at[side]
            )
        )
        copies[-1].start()
    for copy in copies:
        copy.wait()
    for i in range(send_ref.shape[0]):
        send_ref[i] = rows_ref[i % sides]


def table_kernel(
    proj_hbm, weight_hbm, source_hbm, target_hbm, presence_hbm, table_ref, source_ref, target_ref, row_ref, sems, between
):
    width = table_ref.shape[1]
    pairs = [(proj_hbm, table_ref.at[:width]), (source_hbm, source_ref), (target_hbm, target_ref)]
    pairs.append((presence_hbm, row_ref))
    for i in range(weight_hbm.shape[1] // width):
        pairs.append(
            (
                weight_hbm.at[:, i * width : (i + 1) * width],
                table_ref.at[(i + 1) * width : (i + 2) * width],
            )
        )
    copies = [pltpu.make_async_copy(*pair, sems.at[i]) for i, pair in enumerate(pairs)]
    for copy in copies:
        copy.start()
    between()
    for copy in copies:
        copy.wait()
    row = lax.broadcasted_iota(jnp.int32, (16, width), 0)
    block = jnp.zeros((16, width), jnp.float32)
    for i, vector in enumerate(split_rows(source_ref[...]) + split_rows(target_ref[...])):
        block = jnp.where(row == i, vector, block)
    table_ref[3 * width : 3 * width + 16] = block.astype(jnp.bfloat16)
    table_ref[3 * width + 16 :] = jnp.zeros((16, width), jnp.bfloat16)
    table_ref[3 * width + 16 :, : row_ref.shape[1]] = jnp.broadcast_to(
        row_ref[...].astype(jnp.float32), (16, row_ref.shape[1])
    ).astype(jnp.bfloat16)


def prepare_kernel(
    features_hbm, proj_hbm, weight_hbm, source_hbm, target_hbm, presence_hbm,
    send_ref, table_ref, rows_ref, source_ref, target_ref, row_ref, send_sems, table_sems,
):
    table_kernel(
        proj_hbm, weight_hbm, source_hbm, target_hbm, presence_hbm,
        table_ref, source_ref, target_ref, row_ref, table_sems,
        lambda: send_kernel(features_hbm, send_ref, rows_ref, send_sems),
    )


def pick_kernel(presence_ref, near_ref, gathered_ref, out_ref, slots_ref):
    members, slots = out_ref.shape[:2]
    ends = [jnp.int32(0), jnp.int32(0)]
    for tile in range(gathered_ref.shape[0]):
        rows = gathered_ref[tile]
        for i, ref in enumerate((presence_ref, near_ref)):
            slots_ref[i, ends[i]] = rows
            ends[i] = jnp.minimum(ends[i] + ref[0, tile], slots)
    odd = lax.rem(lax.axis_index("x"), 2)
    for member in range(members):
        row = odd ^ (member // 2)
        for k in range(slots):
            out_ref[member, k] = slots_ref[row, k]


def pack_kernel(own_ref, *refs):
    tables, out_ref = refs[:-1], refs[-1]
    lows, slots, part, width = own_ref.shape
    rows = lows * slots * part
    size = tables[0].shape[0]
    out_ref[:rows] = own_ref[...].reshape(rows, width)
    for i, ref in enumerate(tables):
        out_ref[rows + i * size : rows + (i + 1) * size] = ref[...]


def mask_kernel(presence_ref, masks_ref, out_ref):
    _, slots, tile, _ = masks_ref.shape
    node = (lax.axis_index("yh") * SIZES["z"] + lax.axis_index("z")) * SIZES["x"] + lax.axis_index("x")
    for k in range(slots):
        out_ref[k] = jnp.where(masks_ref[0, k] == 1, 0.0, LOW)

    def count(i, rank):
        return rank + presence_ref[0, i]

    rank = lax.fori_loop(0, node, count, jnp.int32(0))

    @pl.when(presence_ref[0, node] == 1)
    def _():
        down = lax.broadcasted_iota(jnp.int32, (tile, tile), 0)
        over = lax.broadcasted_iota(jnp.int32, (tile, tile), 1)
        out_ref[rank] = jnp.where(down == over, LOW, out_ref[rank])


def attend_kernel(own_ref, other_ref, features_ref, added_ref, out_ref, values, tables):
    slots, lows, cores, part, columns = values.shape
    heads, size, width = tables.shape
    tile = added_ref.shape[1]
    share = slots * part
    rows = lows * share
    core = lax.axis_index("c")
    for ref, side in ((own_ref, core), (other_ref, 1 - core)):
        for flip in range(lows):
            start = rows + flip * size
            tables[cores * (lax.axis_index("yl") ^ flip) + side] = ref[start : start + size]
    both = jnp.concatenate([tables[h, :width] for h in range(heads)], axis=1)

    def project(block):
        return jnp.dot(block, both, preferred_element_type=jnp.float32).astype(jnp.bfloat16)

    for ref, side in ((own_ref, core), (other_ref, 1 - core)):
        for low in range(lows):
            block = project(ref[low * share : (low + 1) * share])
            values[:, low, side] = block.reshape(slots, part, columns)

    local = project(features_ref[...]).astype(jnp.float32)
    row = lax.broadcasted_iota(jnp.int32, (8 * heads, width), 0)
    target_terms, self_source, spread = [], [], []
    for h in range(heads):
        wide = tables[h, 3 * width : 3 * width + 16].astype(jnp.float32)
        source = wide[0:1] + wide[1:2] + wide[2:3]
        target = wide[3:4] + wide[4:5] + wide[5:6]
        mine = local[:, h * width : (h + 1) * width]
        target_terms.append(LOG2E * jnp.sum(mine * target, axis=1, keepdims=True))
        self_source.append(LOG2E * jnp.sum(mine * source, axis=1, keepdims=True))
        block = jnp.zeros((8 * heads, width), jnp.float32)
        for i in range(3):
            block = jnp.where(row == 8 * h + i, wide[i : i + 1], block)
        spread.append(block)
    terms = lax.dot_general(
        jnp.concatenate(spread, axis=1).astype(jnp.bfloat16),
        values[...].reshape(slots * tile, columns),
        (((1,), (1,)), ((), ())),
        preferred_element_type=jnp.float32,
    )
    source_terms = [
        LOG2E * (terms[8 * h : 8 * h + 1] + terms[8 * h + 1 : 8 * h + 2] + terms[8 * h + 2 : 8 * h + 3])
        for h in range(heads)
    ]

    best = [jnp.full((tile, tile), LOW, jnp.float32) for h in range(heads)]
    for k in range(slots):
        added = added_ref[k]
        for h in range(heads):
            best[h] = jnp.maximum(best[h], source_terms[h][:, k * tile : (k + 1) * tile] + added)
    peaks, self_weights = [], []
    for h in range(heads):
        top = jnp.maximum(jnp.max(best[h], axis=1, keepdims=True), self_source[h])
        peaks.append(leaky_relu(target_terms[h] + top))
        self_weights.append(jnp.exp2(leaky_relu(target_terms[h] + self_source[h]) - peaks[h]))

    totals = [jnp.zeros((tile, tile), jnp.float32) for h in range(heads)]
    sums = [jnp.zeros((tile, width), jnp.float32) for h in range(heads)]
    group = 2
    for first in range(0, slots, group):
        for h in range(heads):
            edges = []
            for k in range(first, first + group):
                scores = source_terms[h][:, k * tile : (k + 1) * tile] + added_ref[k]
                edge = jnp.exp2(leaky_relu(target_terms[h] + scores) - peaks[h])
                totals[h] = totals[h] + edge
                edges.append(edge.astype(jnp.bfloat16))
            near = values[first : first + group, :, :, :, h * width : (h + 1) * width]
            sums[h] = sums[h] + jnp.dot(
                jnp.concatenate(edges, axis=1),
                near.reshape(group * tile, width),
                preferred_element_type=jnp.float32,
            )

    outs = []
    for h in range(heads):
        mine = local[:, h * width : (h + 1) * width]
        denominator = jnp.sum(totals[h], axis=1, keepdims=True) + self_weights[h]
        summed = sums[h] + self_weights[h].astype(jnp.bfloat16).astype(jnp.float32) * mine
        attended = summed / denominator
        below = jnp.minimum(attended, 0.0)
        bent = jnp.tanh(0.5 * below)
        outs.append(jnp.where(attended > 0, attended, 2.0 * bent / (1.0 - bent)).astype(jnp.bfloat16))
    joined = jnp.concatenate(outs, axis=1)
    columns = []
    for i in (1, 2):
        table = jnp.concatenate(
            [tables[h, i * width : (i + 1) * width] for h in range(heads)], axis=0
        )
        columns.append(jnp.dot(joined, table, preferred_element_type=jnp.float32))
    mixed = jnp.concatenate(columns, axis=1).astype(jnp.bfloat16)
    out_ref[...] = mixed


def per_device(features, proj_weight, score_source, score_target, out_weight, presence, tile_masks):
    tile, width = features.shape
    slots = tile_masks.shape[1]
    part = tile // EIGHTHS
    lows = SIZES["yl"]
    vmem = pl.BlockSpec(memory_space=pltpu.VMEM)
    smem = pl.BlockSpec(memory_space=pltpu.SMEM)
    raw = pl.BlockSpec(memory_space=pltpu.HBM)

    far = [
        pltpu.with_memory_space_constraint(value, pltpu.HBM)
        for value in (features, proj_weight, out_weight, score_source, score_target, presence)
    ]
    size = width + out_weight.shape[1] + 32
    send, table = pl.pallas_call(
        prepare_kernel,
        out_shape=(
            jax.ShapeDtypeStruct((NODES, part, width), jnp.bfloat16),
            jax.ShapeDtypeStruct((size, width), jnp.bfloat16),
        ),
        in_specs=[raw] * 6,
        out_specs=(vmem, vmem),
        scratch_shapes=[
            pltpu.VMEM((2, part, width), jnp.bfloat16),
            pltpu.VMEM(score_source.shape, jnp.float32),
            pltpu.VMEM(score_target.shape, jnp.float32),
            pltpu.VMEM(presence.shape, jnp.int32),
            pltpu.SemaphoreType.DMA((2,)),
            pltpu.SemaphoreType.DMA((6,)),
        ],
        compiler_params=pltpu.CompilerParams(vmem_limit_bytes=4 << 20),
        name="prepare",
    )(*far)
    diagonal = [
        (x * lows + yl, (x ^ 1) * lows + (yl ^ 2)) for x in range(SIZES["x"]) for yl in range(lows)
    ]
    tables = {0: table, 2: lax.ppermute(table, ("x", "yl"), diagonal)}
    for flip in (1, 3):
        tables[flip] = lax.ppermute(table, "yl", [(i, i ^ flip) for i in range(lows)])
    near = tables[2][size - 16 : size - 15, : presence.shape[1]].astype(jnp.int32)
    gathered = lax.all_to_all(
        send, EVERY, 0, 0, tiled=True, axis_index_groups=node_groups()
    )
    gathered, near = lax.optimization_barrier((gathered, near))
    picked = pl.pallas_call(
        pick_kernel,
        out_shape=jax.ShapeDtypeStruct((lows, slots, part, width), jnp.bfloat16),
        in_specs=[smem, smem, vmem],
        out_specs=vmem,
        scratch_shapes=[pltpu.VMEM((2, slots + 1, part, width), jnp.bfloat16)],
        compiler_params=pltpu.CompilerParams(vmem_limit_bytes=4 << 20),
        name="pick",
    )(presence, near, gathered)
    swap = [(0, 1), (1, 0)]
    picked, tables = lax.optimization_barrier((picked, tables))
    own = lax.all_to_all(
        picked, EVERY, 0, 0, tiled=True, axis_index_groups=square_groups()
    )
    packed = pl.pallas_call(
        pack_kernel,
        out_shape=jax.ShapeDtypeStruct((lows * slots * part + 4 * size, width), jnp.bfloat16),
        in_specs=[vmem] * 5,
        out_specs=vmem,
        compiler_params=pltpu.CompilerParams(vmem_limit_bytes=4 << 20),
        name="pack",
    )(own, *[tables[flip] for flip in range(4)])
    other = lax.ppermute(packed, "c", swap)
    cores = SIZES["c"]
    added = pl.pallas_call(
        mask_kernel,
        out_shape=jax.ShapeDtypeStruct((slots, tile, tile), jnp.float32),
        in_specs=[smem, vmem],
        out_specs=vmem,
        compiler_params=pltpu.CompilerParams(vmem_limit_bytes=4 << 20),
        cost_estimate=pl.CostEstimate(flops=slots * tile * tile, bytes_accessed=8 * slots * tile * tile, transcendentals=0),
        name="mask",
    )(presence, tile_masks)
    return pl.pallas_call(
        attend_kernel,
        out_shape=jax.ShapeDtypeStruct((tile, out_weight.shape[1]), jnp.bfloat16),
        in_specs=[vmem] * 4,
        out_specs=vmem,
        scratch_shapes=[
            pltpu.VMEM((slots, lows, cores, part, lows * cores * width), jnp.bfloat16),
            pltpu.VMEM((lows * cores, size, width), jnp.bfloat16),
        ],
        compiler_params=pltpu.CompilerParams(vmem_limit_bytes=16 << 20),
        name="attend",
    )(packed, other, features, added)


def solution(mesh):
    shape = tuple(SIZES[name] for name in NODE + HEAD)
    fine = Mesh(np.asarray(mesh.devices).reshape(shape), NODE + HEAD)
    return jax.shard_map(
        per_device,
        mesh=fine,
        in_specs=(
            P(NODE, None),
            P(None, HEAD),
            P(HEAD, None),
            P(HEAD, None),
            P(HEAD, None),
            P(NODE, None),
            P(NODE, None, None, None),
        ),
        out_specs=P(NODE, None),
        check_vma=False,
    )
```
